128 devices in a mesh: view: 4 (over x), xy: 16 (over z, y), gz: 2 (over core).
Axes of the slice: x: 4, y: 4, z: 4, core: 2. Of those that a mesh axis runs over, the one named last changes fastest.
Arguments:
- estimate: float32 [64, 1024, 128], P('gz', 'xy'), may hold values from 0.5 to 2
- views: bfloat16 [4, 64, 1024, 128], P('view', 'gz', 'xy'), may hold values from 0.19921875 to 3
- shifts: int32 [4, 3], P('view'), may hold values from -32 to 32, as said below
- kernels: float32 [4, 3, 63], P('view'), may hold values from 0.02 to 1
- coverage: int32 [4, 8, 1], replicated, may hold values from 0 to 1, as said below
Outputs:
- refined: float32 [64, 1024, 128], P('gz', 'xy')
The draws below stay inside these ranges and needn't reach their ends.
Inputs may be any that keep to these rules, and one draw needn't show every extreme that they name: `shifts`: both ends -32 and 32 occur in every draw. `coverage`: every block is covered by at least one view.
All inputs are finite; a program needn't handle non-finite values.
Results may differ from the reference program's by a relative error of at most 0.0003.
Values may be sent and summed in bfloat16 or wider, within the bound.
No kernel may reach another device: no remote copies, remote signals or barrier semaphores. Data moves between devices by JAX's collectives and lax.ppermute only.
A program may use at most 64 MiB of HBM per device.

```python
import math
import jax
import jax.numpy as jnp
from jax import lax

TAPS = 63
SHIFT = 32
BLOCK = 128
ITERS = 2
NX = 128
VIEWS = 4
NZ = 64
NY = 1024


def draw_shifts(key, part):
    values = jax.random.randint(key, (VIEWS, 3), -SHIFT, SHIFT + 1).reshape(-1)
    order = jax.random.permutation(jax.random.fold_in(key, 1), VIEWS * 3)
    values = values.at[order[0]].set(SHIFT)
    values = values.at[order[1]].set(-SHIFT)
    return values.reshape(VIEWS, 3).astype(jnp.int32)


def draw_coverage(key, part):
    shape = (VIEWS, NY // BLOCK, NX // BLOCK)
    picks = jax.random.randint(key, shape, 0, 5)
    covered = (picks < 3).astype(jnp.int32)
    forced = jax.random.randint(jax.random.fold_in(key, 7), (NY // BLOCK, NX // BLOCK), 0, VIEWS)
    chosen = (jnp.arange(VIEWS)[:, None, None] == forced[None]).astype(jnp.int32)
    return jnp.maximum(covered, chosen).astype(jnp.int32)


def block_scale(rng, shape, shards, least, top_value):
    def one(axis_at, parts):
        heights = jax.random.uniform(jax.random.fold_in(jax.random.fold_in(rng, 6), axis_at), (parts,), jnp.float32, least / len(shards), top_value / len(shards))
        return jnp.repeat(jnp.exp(heights), shape[axis_at] // parts).reshape((-1,) + (1,) * (len(shape) - axis_at - 1))

    gain = one(*shards[0])
    for cut in shards[1:]:
        gain = gain * one(*cut)
    return gain


def setup_inputs(seed: int = 0) -> dict:
    seeds = jax.random.split(jax.random.key(seed), 6)
    estimate = jnp.clip(0.5 + 1.5 * jax.random.uniform(seeds[0], (NZ, NY, NX), jnp.float32) ** block_scale(seeds[0], (NZ, NY, NX), ((0, 2), (1, 16)), -0.2, 0.2), 0.5, 2.0)
    views = jnp.clip(0.19921875 + 2.8007812 * jax.random.uniform(seeds[1], (VIEWS, NZ, NY, NX), jnp.float32) ** block_scale(seeds[1], (VIEWS, NZ, NY, NX), ((0, 4), (1, 2), (2, 16)), -0.2, 0.2), 0.19921875, 3.0).astype(jnp.bfloat16)
    shifts = draw_shifts(jax.random.fold_in(seeds[5], 71), 0)
    kernels = jnp.clip(jnp.exp(math.log(1.0) - 3.912023 * jax.random.uniform(seeds[3], (VIEWS, 3, TAPS), jnp.float32) ** block_scale(seeds[3], (VIEWS, 3, TAPS), ((0, 4),), -0.2, 0.2)), 0.02, 1.0)
    coverage = draw_coverage(jax.random.fold_in(seeds[5], 71), 0)
    return dict(estimate=estimate, views=views, shifts=shifts, kernels=kernels, coverage=coverage)


def filtered(vol, taps_row, axis):
    half = (TAPS - 1) // 2
    length = vol.shape[axis]
    total = length + TAPS - 1
    spectrum = jnp.fft.rfft(vol, n=total, axis=axis)
    kernel_hat = jnp.fft.rfft(taps_row, n=total)
    shape = [1, 1, 1]
    shape[axis] = kernel_hat.shape[0]
    full = jnp.fft.irfft(spectrum * kernel_hat.reshape(shape), n=total, axis=axis)
    return lax.slice_in_dim(full, half, half + length, axis=axis).astype(vol.dtype)


def separable(vol, psf_view, forward):
    result = vol
    for axis in (2, 1, 0):
        row = psf_view[axis]
        taps_row = row[::-1] if forward else row
        result = filtered(result, taps_row, axis)
    return result


def reference(estimate, views, shifts, kernels, coverage):
    psf = kernels / jnp.sum(kernels, axis=2, keepdims=True)
    weights = jnp.repeat(jnp.repeat(coverage.astype(jnp.float32), BLOCK, axis=1), BLOCK, axis=2)
    count = jnp.sum(weights, axis=0)
    data = []
    for view_id in range(VIEWS):
        padded = jnp.pad(views[view_id].astype(jnp.float32), SHIFT)
        start = (SHIFT + shifts[view_id]).astype(jnp.int32)
        data.append(lax.dynamic_slice(padded, (start[0], start[1], start[2]), (NZ, NY, NX)))
    field = estimate
    for step in range(ITERS):
        total = jnp.zeros_like(field)
        for view_id in range(VIEWS):
            predicted = separable(field, psf[view_id], True)
            ratio = data[view_id] / (predicted + 0.05)
            total = total + weights[view_id][None] * separable(ratio, psf[view_id], False)
        field = field * total / count[None]
    return field
```

```python
import jax
import jax.numpy as jnp
from jax import lax
from jax.experimental import pallas as pl
from jax.experimental.pallas import tpu as pltpu
from jax.sharding import PartitionSpec as P

F32 = jnp.float32
BF16 = jnp.bfloat16
ITERS = 2
VIEWS = 4
PLANES = 64
ROWS = 32
WIDTH = 128
SPAN = 3 * ROWS
QUARTER = ROWS // VIEWS
FLAT = ROWS * PLANES
QFLAT = QUARTER * PLANES
HALF = 31
BLOCK = 128
STRIPS = ("xy", "gz")


def dot(a, b):
    return jnp.dot(a, b, preferred_element_type=F32)


def split(x):
    high = x.astype(BF16)
    return high, (x - high.astype(F32)).astype(BF16)


def call(kernel, outs, scratch=(), flops=10**8, smem=()):
    def run(*args):
        n = len(args)
        specs = [
            pl.BlockSpec(memory_space=pltpu.SMEM if i in smem else pltpu.VMEM) for i in range(n)
        ]
        one = not isinstance(outs, (list, tuple))
        shapes = [outs] if one else list(outs)
        made = pl.pallas_call(
            kernel,
            out_shape=shapes,
            in_specs=specs,
            out_specs=[pl.BlockSpec(memory_space=pltpu.VMEM)] * len(shapes),
            scratch_shapes=list(scratch),
            cost_estimate=pl.CostEstimate(flops=flops, bytes_accessed=4 << 20, transcendentals=0),
        )(*args)
        return made[0] if one else made

    return run


def arr(shape, dtype):
    return jax.ShapeDtypeStruct(shape, dtype)


def strip_index():
    return lax.axis_index("xy") * 2 + lax.axis_index("gz")


def prep_kernel(est, views, eb, em, eo, vm, vo, mine, theirs):
    v, g = lax.axis_index("view"), lax.axis_index("gz")
    eb[...] = est[...].astype(BF16)

    def cut(first, second):
        em[...] = est[:, first : first + ROWS, :].astype(BF16)
        eo[...] = est[:, second : second + ROWS, :].astype(BF16)
        vm[...] = views[0, :, first : first + ROWS, :]
        vo[...] = views[0, :, second : second + ROWS, :]

    @pl.when(g == 0)
    def _():
        cut(0, ROWS)

    @pl.when(g == 1)
    def _():
        cut(ROWS, 0)

    here = pl.multiple_of(g * ROWS + v * QUARTER, QUARTER)
    there = pl.multiple_of((1 - g) * ROWS + v * QUARTER, QUARTER)
    mine[...] = est[:, pl.ds(here, QUARTER), :]
    theirs[...] = est[:, pl.ds(there, QUARTER), :]


def toeplitz(row, rows, shift):
    return pltpu.roll(jnp.broadcast_to(row, (rows, WIDTH)), shift, 1, stride=1, stride_axis=0)


def normed(taps):
    return taps / jnp.sum(taps, axis=1, keepdims=True)


def x_matrix(row):
    i = lax.broadcasted_iota(jnp.int32, (WIDTH, WIDTH), 0)
    j = lax.broadcasted_iota(jnp.int32, (WIDTH, WIDTH), 1)
    full = toeplitz(row, WIDTH, WIDTH - HALF)
    return jnp.where(jnp.abs(i - j) <= HALF, full, 0.0)


def row_valid(rows):
    r = strip_index()
    j = lax.broadcasted_iota(jnp.int32, (rows, WIDTH), 1)
    low = jnp.where(r == 0, ROWS, 0)
    high = jnp.where(r == 2 * lax.axis_size("xy") - 1, 2 * ROWS, SPAN)
    return (j >= low) & (j < high)


def own_mats_kernel(taps, shifts, yf, yb, zf, x1f, x2f, yd, zd, xd):
    k = normed(taps[...])
    valid = row_valid(ROWS)
    for ref, row in ((yf, 1), (yb, 4)):
        h, l = split(jnp.where(valid, toeplitz(k[row : row + 1], ROWS, 1), 0.0))
        ref[0:ROWS, :] = h
        ref[ROWS : 2 * ROWS, :] = l
    lane = lax.broadcasted_iota(jnp.int32, (PLANES, WIDTH), 1)
    z = jnp.where(lane < PLANES, toeplitz(k[0:1], PLANES, WIDTH - HALF), 0.0)
    zh = z.astype(BF16).astype(F32)
    zf[0:PLANES, :] = (zh + pltpu.roll(zh, PLANES, 1)).astype(BF16)
    zf[PLANES : 2 * PLANES, :] = (z - zh).astype(BF16)
    h, l = split(x_matrix(k[5:6]))
    x1f[0:WIDTH, :] = h
    x1f[WIDTH : 2 * WIDTH, :] = h
    x2f[...] = l

    def hot(rows, offset):
        i = lax.broadcasted_iota(jnp.int32, (rows, WIDTH), 0)
        j = lax.broadcasted_iota(jnp.int32, (rows, WIDTH), 1)
        return jnp.where(j - i == offset, 1.0, 0.0)

    yd[...] = jnp.where(valid, hot(ROWS, shifts[0, 1] + ROWS), 0.0).astype(BF16)
    zd[...] = hot(PLANES, shifts[0, 0]).astype(BF16)
    xd[...] = hot(WIDTH, -shifts[0, 2]).astype(BF16)


def all_mats_kernel(t0, t1, t2, t3, zb, x1b, x2b):
    for i, taps in enumerate((t0, t1, t2, t3)):
        k = normed(taps[...])
        zh, zl = split(toeplitz(k[3:4], PLANES, WIDTH - HALF))
        zb[i, 0:PLANES, :] = zh
        zb[i, PLANES : 2 * PLANES, :] = zl
        h, l = split(x_matrix(k[2:3]))
        x1b[i, 0:WIDTH, :] = h
        x1b[i, WIDTH : 2 * WIDTH, :] = h
        x2b[i] = l


def y_stage(pair, matrix, t):
    def body(c, carry):
        for u in range(8):
            p = c * 16 + 2 * u
            o = dot(matrix, pair(p))
            if matrix.shape[0] == 2 * ROWS:
                o = o[0:ROWS] + o[ROWS : 2 * ROWS]
            t[pl.ds(p * ROWS, ROWS), :] = o[:, 0:WIDTH]
            t[pl.ds(p * ROWS + ROWS, ROWS), :] = o[:, WIDTH : 2 * WIDTH]
        return carry

    lax.fori_loop(0, PLANES // 16, body, 0)


def zx_stage(t, zf, x1, x2, hl, emit):
    def body(c, carry):
        for u in range(4):
            r = c * 8 + 2 * u
            h0, l0 = split(t[pl.ds(r, PLANES, stride=ROWS), :])
            h1, l1 = split(t[pl.ds(r + 1, PLANES, stride=ROWS), :])
            rhs = jnp.concatenate(
                [jnp.concatenate([h0, h1], axis=1), jnp.concatenate([l0, l1], axis=1)], axis=0
            )
            o = dot(zf, rhs)
            zh, zl = split(o[0:PLANES] + o[PLANES : 2 * PLANES])
            at = 2 * u * PLANES
            hl[at : at + PLANES, 0:WIDTH] = zh[:, 0:WIDTH]
            hl[at : at + PLANES, WIDTH : 2 * WIDTH] = zl[:, 0:WIDTH]
            at = at + PLANES
            hl[at : at + PLANES, 0:WIDTH] = zh[:, WIDTH : 2 * WIDTH]
            hl[at : at + PLANES, WIDTH : 2 * WIDTH] = zl[:, WIDTH : 2 * WIDTH]
        emit(c, dot(hl[...], x1) + dot(hl[:, 0:WIDTH], x2))
        return carry

    lax.fori_loop(0, ROWS // 8, body, 0)


def gather_first(f, slab, other, far_a, far_b):
    g = lax.axis_index("gz")
    low, high = slice(0, PLANES // 2), slice(PLANES // 2, PLANES)

    @pl.when(g == 0)
    def _():
        f[low, ROWS:SPAN, :] = slab[...]
        f[high, ROWS:SPAN, :] = other[...]
        f[low, 0:ROWS, :] = far_a[...]
        f[high, 0:ROWS, :] = far_b[...]

    @pl.when(g == 1)
    def _():
        f[high, 0 : 2 * ROWS, :] = slab[...]
        f[low, 0 : 2 * ROWS, :] = other[...]
        f[high, 2 * ROWS : SPAN, :] = far_a[...]
        f[low, 2 * ROWS : SPAN, :] = far_b[...]


def window_pair(f):
    return lambda p: jnp.concatenate([f[p], f[p + 1]], axis=1)


def first_pred_kernel(slab, other, far_a, far_b, yf, zf, x1, x2, pred, f, t, hl):
    gather_first(f, slab, other, far_a, far_b)
    y_stage(window_pair(f), yf[:, 0:SPAN], t)

    def emit(c, x):
        pred[pl.ds(c * QFLAT, QFLAT), :] = x

    zx_stage(t, zf[...], x1[...], x2[...], hl, emit)


def first_ratio_kernel(slab, other, far_a, far_b, yd, zd, xd, pred, data, ratio, f, t, hl):
    gather_first(f, slab, other, far_a, far_b)
    y_stage(window_pair(f), yd[:, 0:SPAN], t)
    zmat = zd[:, 0:PLANES]

    def body(c, carry):
        for u in range(4):
            r = c * 8 + 2 * u
            h0 = t[pl.ds(r, PLANES, stride=ROWS), :].astype(BF16)
            h1 = t[pl.ds(r + 1, PLANES, stride=ROWS), :].astype(BF16)
            o = dot(zmat, jnp.concatenate([h0, h1], axis=1)).astype(BF16)
            at = 2 * u * PLANES
            hl[at : at + PLANES, 0:WIDTH] = o[:, 0:WIDTH]
            hl[at + PLANES : at + 2 * PLANES, 0:WIDTH] = o[:, WIDTH : 2 * WIDTH]
        d = dot(hl[:, 0:WIDTH], xd[...])
        at = pl.ds(c * QFLAT, QFLAT)
        data[at, :] = d.astype(BF16)
        ratio[at, :] = (d / (pred[at, :] + 0.05)).astype(BF16)
        return carry

    lax.fori_loop(0, ROWS // 8, body, 0)


def strided_pair(s):
    def pair(p):
        a = s[pl.ds(p, SPAN, stride=PLANES), :].astype(BF16)
        b = s[pl.ds(p + 1, SPAN, stride=PLANES), :].astype(BF16)
        return jnp.concatenate([a, b], axis=1)

    return pair


def back_y_kernel(low, own, high, yb, o0, o1, o2, o3, s, t):
    for i, ref in enumerate((low, own, high)):
        s[i * FLAT : (i + 1) * FLAT, :] = ref[...].astype(F32)
    y_stage(strided_pair(s), yb[:, 0:SPAN], t)
    v = lax.axis_index("view")
    for i, out in enumerate((o0, o1, o2, o3)):
        q = lax.rem(v + i, VIEWS) * QUARTER
        for r in range(QUARTER):
            out[r * PLANES : (r + 1) * PLANES, :] = t[
                pl.ds(q + r, PLANES, stride=ROWS), :
            ].astype(BF16)


def next_ratio_kernel(low, own, high, yf, zf, x1, x2, data, ratio, s, t, hl):
    v = lax.axis_index("view")
    for i, ref in enumerate((low, own, high)):
        for j in range(VIEWS):
            q = lax.rem(v - j + VIEWS, VIEWS)
            at = pl.multiple_of(i * FLAT + q * QFLAT, QFLAT)
            s[pl.ds(at, QFLAT), :] = ref[j * QFLAT : (j + 1) * QFLAT, :].astype(F32)
    y_stage(strided_pair(s), yf[:, 0:SPAN], t)

    def emit(c, x):
        at = pl.ds(c * QFLAT, QFLAT)
        ratio[at, :] = (data[at, :].astype(F32) / (x + 0.05)).astype(BF16)

    zx_stage(t, zf[...], x1[...], x2[...], hl, emit)


def weighted_total(terms, coverage, zb, x1b, x2b, hl, acc):
    v = lax.axis_index("view")
    block = strip_index() * ROWS // BLOCK
    count = coverage[0, block, 0]
    for w in range(1, VIEWS):
        count = count + coverage[w, block, 0]
    for i, term in enumerate(terms):
        weight = coverage[lax.rem(v - i + VIEWS, VIEWS), block, 0].astype(F32)
        zmat = zb[i, :, 0:PLANES]
        for u in range(QUARTER // 2):
            at = 2 * u * PLANES
            rhs = jnp.concatenate(
                [term[at : at + PLANES, :], term[at + PLANES : at + 2 * PLANES, :]], axis=1
            )
            o = dot(zmat, rhs)
            zh, zl = split(o[0:PLANES] + o[PLANES : 2 * PLANES])
            hl[at : at + PLANES, 0:WIDTH] = zh[:, 0:WIDTH]
            hl[at : at + PLANES, WIDTH : 2 * WIDTH] = zl[:, 0:WIDTH]
            at = at + PLANES
            hl[at : at + PLANES, 0:WIDTH] = zh[:, WIDTH : 2 * WIDTH]
            hl[at : at + PLANES, WIDTH : 2 * WIDTH] = zl[:, WIDTH : 2 * WIDTH]
        got = weight * (dot(hl[...], x1b[i]) + dot(hl[:, 0:WIDTH], x2b[i]))
        acc[...] = got if i == 0 else acc[...] + got
    return count.astype(F32)


def first_update_kernel(
    t0, t1, t2, t3, coverage, mine, theirs, zb, x1b, x2b, field, sent, hl, acc, fq
):
    g = lax.axis_index("gz")
    half = QFLAT // 2

    @pl.when(g == 0)
    def _():
        fq[0:half, :] = mine[...]
        fq[half:QFLAT, :] = theirs[...]

    @pl.when(g == 1)
    def _():
        fq[half:QFLAT, :] = mine[...]
        fq[0:half, :] = theirs[...]

    count = weighted_total((t0, t1, t2, t3), coverage, zb, x1b, x2b, hl, acc)
    for r in range(QUARTER):
        at = slice(r * PLANES, (r + 1) * PLANES)
        new = fq[pl.ds(r, PLANES, stride=QUARTER), :] * acc[at, :] / count
        field[at, :] = new
        sent[at, :] = new.astype(BF16)


def last_update_kernel(t0, t1, t2, t3, coverage, old, zb, x1b, x2b, field, hl, acc):
    count = weighted_total((t0, t1, t2, t3), coverage, zb, x1b, x2b, hl, acc)
    field[...] = old[...] * acc[...] / count


def halves_kernel(p0, p1, p2, p3, keep, give):
    v, g = lax.axis_index("view"), lax.axis_index("gz")
    half = PLANES // 2
    for j, ref in enumerate((p0, p1, p2, p3)):
        q = lax.rem(v - j + VIEWS, VIEWS) * QUARTER
        for r in range(QUARTER):
            at = pl.multiple_of((q + r) * half, half)
            a = pl.multiple_of(r * PLANES + g * half, half)
            b = pl.multiple_of(r * PLANES + (1 - g) * half, half)
            keep[pl.ds(at, half), :] = ref[pl.ds(a, half), :]
            give[pl.ds(at, half), :] = ref[pl.ds(b, half), :]


def final_kernel(keep, got, out):
    g = lax.axis_index("gz")
    half = PLANES // 2

    def put(first, second):
        for p in range(half):
            out[p, 0:ROWS, :] = first[pl.ds(p, ROWS, stride=half), :]
            out[p, ROWS : 2 * ROWS, :] = second[pl.ds(p, ROWS, stride=half), :]

    @pl.when(g == 0)
    def _():
        put(keep, got)

    @pl.when(g == 1)
    def _():
        put(got, keep)


def steps(count, shift):
    return [(i, (i + shift) % count) for i in range(count)]


def on_device(estimate, views, shifts, kernels, coverage):
    strips = lax.axis_size("xy")
    count = 2 * strips
    half = PLANES // 2
    quart = (QFLAT, WIDTH)
    both = [kernels[0], kernels[0][:, ::-1]]
    taps = jnp.pad(jnp.concatenate(both, axis=0), ((0, 2), (0, WIDTH - kernels.shape[2])))

    eb, em, eo, vm, vo, mine, theirs = call(
        prep_kernel,
        [
            arr((half, 2 * ROWS, WIDTH), BF16),
            arr((half, ROWS, WIDTH), BF16),
            arr((half, ROWS, WIDTH), BF16),
            arr((half, ROWS, WIDTH), BF16),
            arr((half, ROWS, WIDTH), BF16),
            arr((half, QUARTER, WIDTH), F32),
            arr((half, QUARTER, WIDTH), F32),
        ],
    )(estimate, views)

    outward, inward = [], []
    for s in range(strips):
        outward += [(2 * s, 2 * ((s + 1) % strips)), (2 * s + 1, 2 * ((s - 1) % strips) + 1)]
        inward += [(2 * s, 2 * ((s - 1) % strips) + 1), (2 * s + 1, 2 * ((s + 1) % strips))]
    swap = steps(2, 1)
    e_far = [lax.ppermute(eo, STRIPS, outward), lax.ppermute(em, STRIPS, inward)]
    e_all = [eb, lax.ppermute(eb, "gz", swap)] + e_far
    v_far = [lax.ppermute(vo, STRIPS, outward), lax.ppermute(vm, STRIPS, inward)]
    v_all = [views[0], lax.ppermute(views[0], "gz", swap)] + v_far
    theirs = lax.ppermute(theirs, "gz", swap)
    every = [taps] + [lax.ppermute(taps, "view", steps(VIEWS, i)) for i in range(1, VIEWS)]

    yf, yb, zf, x1f, x2f, yd, zd, xd = call(
        own_mats_kernel,
        [
            arr((2 * ROWS, WIDTH), BF16),
            arr((2 * ROWS, WIDTH), BF16),
            arr((2 * PLANES, WIDTH), BF16),
            arr((2 * WIDTH, WIDTH), BF16),
            arr((WIDTH, WIDTH), BF16),
            arr((ROWS, WIDTH), BF16),
            arr((PLANES, WIDTH), BF16),
            arr((WIDTH, WIDTH), BF16),
        ],
        smem=(1,),
    )(taps, shifts)
    zb, x1b, x2b = call(
        all_mats_kernel,
        [
            arr((VIEWS, 2 * PLANES, WIDTH), BF16),
            arr((VIEWS, 2 * WIDTH, WIDTH), BF16),
            arr((VIEWS, WIDTH, WIDTH), BF16),
        ],
    )(*every)

    window = pltpu.VMEM((PLANES, SPAN, WIDTH), BF16)
    wide = pltpu.VMEM((SPAN * PLANES, WIDTH), F32)
    flat = pltpu.VMEM((FLAT, WIDTH), F32)
    pairs = pltpu.VMEM((QFLAT, 2 * WIDTH), BF16)
    total = pltpu.VMEM(quart, F32)

    pred = call(first_pred_kernel, arr((FLAT, WIDTH), F32), [window, flat, pairs])(
        *e_all, yf, zf, x1f, x2f
    )
    data, ratio = call(
        first_ratio_kernel, [arr((FLAT, WIDTH), BF16)] * 2, [window, flat, pairs]
    )(*v_all, yd, zd, xd, pred)

    def neighbours(x):
        return lax.ppermute(x, STRIPS, steps(count, 1)), lax.ppermute(x, STRIPS, steps(count, -1))

    field = None
    for step in range(ITERS):
        low, high = neighbours(ratio)
        parts = call(back_y_kernel, [arr(quart, BF16)] * VIEWS, [wide, flat])(low, ratio, high, yb)
        terms = [parts[0]] + [
            lax.ppermute(parts[i], "view", steps(VIEWS, i)) for i in range(1, VIEWS)
        ]
        if step == 0:
            field, sent = call(
                first_update_kernel,
                [arr(quart, F32), arr(quart, BF16)],
                [pairs, total, total],
                smem=(4,),
            )(
                *terms,
                coverage,
                mine.reshape(QFLAT // 2, WIDTH),
                theirs.reshape(QFLAT // 2, WIDTH),
                zb,
                x1b,
                x2b,
            )
            own = jnp.concatenate(
                [sent] + [lax.ppermute(sent, "view", steps(VIEWS, i)) for i in range(1, VIEWS)],
                axis=0,
            )
            low, high = neighbours(own)
            ratio = call(next_ratio_kernel, arr((FLAT, WIDTH), BF16), [wide, flat, pairs])(
                low, own, high, yf, zf, x1f, x2f, data
            )
        else:
            field = call(last_update_kernel, arr(quart, F32), [pairs, total], smem=(4,))(
                *terms, coverage, field, zb, x1b, x2b
            )
    pieces = [field] + [lax.ppermute(field, "view", steps(VIEWS, i)) for i in range(1, VIEWS)]
    keep, give = call(halves_kernel, [arr((ROWS * half, WIDTH), F32)] * 2)(*pieces)
    got = lax.ppermute(give, "gz", swap)
    return call(final_kernel, arr((half, 2 * ROWS, WIDTH), F32))(keep, got)


def solution(mesh):
    placed = (
        P("gz", "xy", None),
        P("view", "gz", "xy", None),
        P("view", None),
        P("view", None, None),
        P(),
    )
    return jax.shard_map(
        on_device, mesh=mesh, in_specs=placed, out_specs=P("gz", "xy", None), check_vma=False
    )
```

```python
import jax
import jax.numpy as jnp
from jax import lax
from jax.experimental import pallas as pl
from jax.experimental.pallas import tpu as pltpu
from jax.sharding import PartitionSpec as P

F32 = jnp.float32
BF16 = jnp.bfloat16
ITERS = 2
VIEWS = 4
PLANES = 64
ROWS = 32
WIDTH = 128
SPAN = 3 * ROWS
QUARTER = ROWS // VIEWS
FLAT = ROWS * PLANES
QFLAT = QUARTER * PLANES
HALF = 31
BLOCK = 128
STRIPS = ("xy", "gz")


def dot(a, b):
    return jnp.dot(a, b, preferred_element_type=F32)


def split(x):
    high = x.astype(BF16)
    return high, (x - high.astype(F32)).astype(BF16)


def call(kernel, outs, scratch=(), flops=10**8, smem=()):
    def run(*args):
        n = len(args)
        specs = [
            pl.BlockSpec(memory_space=pltpu.SMEM if i in smem else pltpu.VMEM) for i in range(n)
        ]
        one = not isinstance(outs, (list, tuple))
        shapes = [outs] if one else list(outs)
        made = pl.pallas_call(
            kernel,
            out_shape=shapes,
            in_specs=specs,
            out_specs=[pl.BlockSpec(memory_space=pltpu.VMEM)] * len(shapes),
            scratch_shapes=list(scratch),
            compiler_params=pltpu.CompilerParams(vmem_limit_bytes=16 << 20),
            cost_estimate=pl.CostEstimate(flops=flops, bytes_accessed=4 << 20, transcendentals=0),
        )(*args)
        return made[0] if one else made

    return run


def arr(shape, dtype):
    return jax.ShapeDtypeStruct(shape, dtype)


def strip_index():
    return lax.axis_index("xy") * 2 + lax.axis_index("gz")


def prep_kernel(est, views, eb, em, eo, vm, vo, mine, theirs):
    v, g = lax.axis_index("view"), lax.axis_index("gz")
    eb[...] = est[...].astype(BF16)

    def cut(first, second):
        em[...] = est[:, first : first + ROWS, :].astype(BF16)
        eo[...] = est[:, second : second + ROWS, :].astype(BF16)
        vm[...] = views[0, :, first : first + ROWS, :]
        vo[...] = views[0, :, second : second + ROWS, :]

    @pl.when(g == 0)
    def _():
        cut(0, ROWS)

    @pl.when(g == 1)
    def _():
        cut(ROWS, 0)

    here = pl.multiple_of(g * ROWS + v * QUARTER, QUARTER)
    there = pl.multiple_of((1 - g) * ROWS + v * QUARTER, QUARTER)
    mine[...] = est[:, pl.ds(here, QUARTER), :]
    theirs[...] = est[:, pl.ds(there, QUARTER), :]


def toeplitz(row, rows, shift):
    return pltpu.roll(jnp.broadcast_to(row, (rows, WIDTH)), shift, 1, stride=1, stride_axis=0)


def normed(taps):
    return taps / jnp.sum(taps, axis=1, keepdims=True)


def x_matrix(row):
    i = lax.broadcasted_iota(jnp.int32, (WIDTH, WIDTH), 0)
    j = lax.broadcasted_iota(jnp.int32, (WIDTH, WIDTH), 1)
    full = toeplitz(row, WIDTH, WIDTH - HALF)
    return jnp.where(jnp.abs(i - j) <= HALF, full, 0.0)


def row_valid(rows):
    r = strip_index()
    j = lax.broadcasted_iota(jnp.int32, (rows, WIDTH), 1)
    low = jnp.where(r == 0, ROWS, 0)
    high = jnp.where(r == 2 * lax.axis_size("xy") - 1, 2 * ROWS, SPAN)
    return (j >= low) & (j < high)


def own_mats_kernel(taps, shifts, yf, yb, zf, x1f, x2f, yd, zd, xd):
    k = normed(taps[...])
    valid = row_valid(ROWS)
    for ref, row in ((yf, 1), (yb, 4)):
        h, l = split(jnp.where(valid, toeplitz(k[row : row + 1], ROWS, 1), 0.0))
        ref[0:ROWS, :] = h
        ref[ROWS : 2 * ROWS, :] = l
    lane = lax.broadcasted_iota(jnp.int32, (PLANES, WIDTH), 1)
    z = jnp.where(lane < PLANES, toeplitz(k[0:1], PLANES, WIDTH - HALF), 0.0)
    zh = z.astype(BF16).astype(F32)
    zf[0:PLANES, :] = (zh + pltpu.roll(zh, PLANES, 1)).astype(BF16)
    zf[PLANES : 2 * PLANES, :] = (z - zh).astype(BF16)
    h, l = split(x_matrix(k[5:6]))
    x1f[0:WIDTH, :] = h
    x1f[WIDTH : 2 * WIDTH, :] = h
    x2f[...] = l

    def hot(rows, offset):
        i = lax.broadcasted_iota(jnp.int32, (rows, WIDTH), 0)
        j = lax.broadcasted_iota(jnp.int32, (rows, WIDTH), 1)
        return jnp.where(j - i == offset, 1.0, 0.0)

    yd[...] = jnp.where(valid, hot(ROWS, shifts[0, 1] + ROWS), 0.0).astype(BF16)
    zd[...] = hot(PLANES, shifts[0, 0]).astype(BF16)
    xd[...] = hot(WIDTH, -shifts[0, 2]).astype(BF16)


def all_mats_kernel(t0, t1, t2, t3, zb, x1b, x2b):
    for i, taps in enumerate((t0, t1, t2, t3)):
        k = normed(taps[...])
        zh, zl = split(toeplitz(k[3:4], PLANES, WIDTH - HALF))
        zb[i, 0:PLANES, :] = zh
        zb[i, PLANES : 2 * PLANES, :] = zl
        h, l = split(x_matrix(k[2:3]))
        x1b[i, 0:WIDTH, :] = h
        x1b[i, WIDTH : 2 * WIDTH, :] = h
        x2b[i] = l


def y_stage(pair, matrix, t):
    def body(c, carry):
        for u in range(8):
            p = c * 16 + 2 * u
            o = dot(matrix, pair(p))
            if matrix.shape[0] == 2 * ROWS:
                o = o[0:ROWS] + o[ROWS : 2 * ROWS]
            t[pl.ds(p * ROWS, ROWS), :] = o[:, 0:WIDTH]
            t[pl.ds(p * ROWS + ROWS, ROWS), :] = o[:, WIDTH : 2 * WIDTH]
        return carry

    lax.fori_loop(0, PLANES // 16, body, 0)


def zx_stage(t, zf, x1, x2, hl, emit):
    def body(c, carry):
        for u in range(4):
            r = c * 8 + 2 * u
            h0, l0 = split(t[pl.ds(r, PLANES, stride=ROWS), :])
            h1, l1 = split(t[pl.ds(r + 1, PLANES, stride=ROWS), :])
            rhs = jnp.concatenate(
                [jnp.concatenate([h0, h1], axis=1), jnp.concatenate([l0, l1], axis=1)], axis=0
            )
            o = dot(zf, rhs)
            zh, zl = split(o[0:PLANES] + o[PLANES : 2 * PLANES])
            at = 2 * u * PLANES
            hl[at : at + PLANES, 0:WIDTH] = zh[:, 0:WIDTH]
            hl[at : at + PLANES, WIDTH : 2 * WIDTH] = zl[:, 0:WIDTH]
            at = at + PLANES
            hl[at : at + PLANES, 0:WIDTH] = zh[:, WIDTH : 2 * WIDTH]
            hl[at : at + PLANES, WIDTH : 2 * WIDTH] = zl[:, WIDTH : 2 * WIDTH]
        emit(c, dot(hl[...], x1) + dot(hl[:, 0:WIDTH], x2))
        return carry

    lax.fori_loop(0, ROWS // 8, body, 0)


def gather_first(f, slab, other, far_a, far_b):
    g = lax.axis_index("gz")
    low, high = slice(0, PLANES // 2), slice(PLANES // 2, PLANES)

    @pl.when(g == 0)
    def _():
        f[low, ROWS:SPAN, :] = slab[...]
        f[high, ROWS:SPAN, :] = other[...]
        f[low, 0:ROWS, :] = far_a[...]
        f[high, 0:ROWS, :] = far_b[...]

    @pl.when(g == 1)
    def _():
        f[high, 0 : 2 * ROWS, :] = slab[...]
        f[low, 0 : 2 * ROWS, :] = other[...]
        f[high, 2 * ROWS : SPAN, :] = far_a[...]
        f[low, 2 * ROWS : SPAN, :] = far_b[...]


def window_pair(f):
    return lambda p: jnp.concatenate([f[p], f[p + 1]], axis=1)


def first_pred_kernel(slab, other, far_a, far_b, yf, zf, x1, x2, pred, f, t, hl):
    gather_first(f, slab, other, far_a, far_b)
    y_stage(window_pair(f), yf[:, 0:SPAN], t)

    def emit(c, x):
        pred[pl.ds(c * QFLAT, QFLAT), :] = x

    zx_stage(t, zf[...], x1[...], x2[...], hl, emit)


def first_ratio_kernel(slab, other, far_a, far_b, yd, zd, xd, pred, data, ratio, f, t, hl):
    gather_first(f, slab, other, far_a, far_b)
    y_stage(window_pair(f), yd[:, 0:SPAN], t)
    zmat = zd[:, 0:PLANES]

    def body(c, carry):
        for u in range(4):
            r = c * 8 + 2 * u
            h0 = t[pl.ds(r, PLANES, stride=ROWS), :].astype(BF16)
            h1 = t[pl.ds(r + 1, PLANES, stride=ROWS), :].astype(BF16)
            o = dot(zmat, jnp.concatenate([h0, h1], axis=1)).astype(BF16)
            at = 2 * u * PLANES
            hl[at : at + PLANES, 0:WIDTH] = o[:, 0:WIDTH]
            hl[at + PLANES : at + 2 * PLANES, 0:WIDTH] = o[:, WIDTH : 2 * WIDTH]
        d = dot(hl[:, 0:WIDTH], xd[...])
        at = pl.ds(c * QFLAT, QFLAT)
        data[at, :] = d.astype(BF16)
        ratio[at, :] = (d / (pred[at, :] + 0.05)).astype(BF16)
        return carry

    lax.fori_loop(0, ROWS // 8, body, 0)


def strided_pair(s):
    def pair(p):
        a = s[pl.ds(p, SPAN, stride=PLANES), :].astype(BF16)
        b = s[pl.ds(p + 1, SPAN, stride=PLANES), :].astype(BF16)
        return jnp.concatenate([a, b], axis=1)

    return pair


def back_y_kernel(low, own, high, yb, o0, o1, o2, o3, s, t):
    for i, ref in enumerate((low, own, high)):
        s[i * FLAT : (i + 1) * FLAT, :] = ref[...].astype(F32)
    y_stage(strided_pair(s), yb[:, 0:SPAN], t)
    v = lax.axis_index("view")
    for i, out in enumerate((o0, o1, o2, o3)):
        q = lax.rem(v + i, VIEWS) * QUARTER
        for r in range(QUARTER):
            out[r * PLANES : (r + 1) * PLANES, :] = t[
                pl.ds(q + r, PLANES, stride=ROWS), :
            ].astype(BF16)


def next_ratio_kernel(low, own, high, yf, zf, x1, x2, data, ratio, s, t, hl):
    v = lax.axis_index("view")
    for i, ref in enumerate((low, own, high)):
        for j in range(VIEWS):
            q = lax.rem(v - j + VIEWS, VIEWS)
            at = pl.multiple_of(i * FLAT + q * QFLAT, QFLAT)
            s[pl.ds(at, QFLAT), :] = ref[j * QFLAT : (j + 1) * QFLAT, :].astype(F32)
    y_stage(strided_pair(s), yf[:, 0:SPAN], t)

    def emit(c, x):
        at = pl.ds(c * QFLAT, QFLAT)
        ratio[at, :] = (data[at, :].astype(F32) / (x + 0.05)).astype(BF16)

    zx_stage(t, zf[...], x1[...], x2[...], hl, emit)


def weighted_total(terms, coverage, zb, x1b, x2b, hl, acc):
    v = lax.axis_index("view")
    block = strip_index() * ROWS // BLOCK
    count = coverage[0, block, 0]
    for w in range(1, VIEWS):
        count = count + coverage[w, block, 0]
    for i, term in enumerate(terms):
        weight = coverage[lax.rem(v - i + VIEWS, VIEWS), block, 0].astype(F32)
        zmat = zb[i, :, 0:PLANES]
        for u in range(QUARTER // 2):
            at = 2 * u * PLANES
            rhs = jnp.concatenate(
                [term[at : at + PLANES, :], term[at + PLANES : at + 2 * PLANES, :]], axis=1
            )
            o = dot(zmat, rhs)
            zh, zl = split(o[0:PLANES] + o[PLANES : 2 * PLANES])
            hl[at : at + PLANES, 0:WIDTH] = zh[:, 0:WIDTH]
            hl[at : at + PLANES, WIDTH : 2 * WIDTH] = zl[:, 0:WIDTH]
            at = at + PLANES
            hl[at : at + PLANES, 0:WIDTH] = zh[:, WIDTH : 2 * WIDTH]
            hl[at : at + PLANES, WIDTH : 2 * WIDTH] = zl[:, WIDTH : 2 * WIDTH]
        got = weight * (dot(hl[...], x1b[i]) + dot(hl[:, 0:WIDTH], x2b[i]))
        acc[...] = got if i == 0 else acc[...] + got
    return count.astype(F32)


def first_update_kernel(
    t0, t1, t2, t3, coverage, mine, theirs, zb, x1b, x2b, field, sent, hl, acc, fq
):
    g = lax.axis_index("gz")
    half = QFLAT // 2

    @pl.when(g == 0)
    def _():
        fq[0:half, :] = mine[...]
        fq[half:QFLAT, :] = theirs[...]

    @pl.when(g == 1)
    def _():
        fq[half:QFLAT, :] = mine[...]
        fq[0:half, :] = theirs[...]

    count = weighted_total((t0, t1, t2, t3), coverage, zb, x1b, x2b, hl, acc)
    for r in range(QUARTER):
        at = slice(r * PLANES, (r + 1) * PLANES)
        new = fq[pl.ds(r, PLANES, stride=QUARTER), :] * acc[at, :] / count
        field[at, :] = new
        sent[at, :] = new.astype(BF16)


def last_update_kernel(t0, t1, t2, t3, coverage, old, zb, x1b, x2b, field, hl, acc):
    count = weighted_total((t0, t1, t2, t3), coverage, zb, x1b, x2b, hl, acc)
    field[...] = old[...] * acc[...] / count


def halves_kernel(p0, p1, p2, p3, keep, give):
    v, g = lax.axis_index("view"), lax.axis_index("gz")
    half = PLANES // 2
    for j, ref in enumerate((p0, p1, p2, p3)):
        q = lax.rem(v - j + VIEWS, VIEWS) * QUARTER
        for r in range(QUARTER):
            at = pl.multiple_of((q + r) * half, half)
            a = pl.multiple_of(r * PLANES + g * half, half)
            b = pl.multiple_of(r * PLANES + (1 - g) * half, half)
            keep[pl.ds(at, half), :] = ref[pl.ds(a, half), :]
            give[pl.ds(at, half), :] = ref[pl.ds(b, half), :]


def final_kernel(keep, got, out):
    g = lax.axis_index("gz")
    half = PLANES // 2

    def put(first, second):
        for p in range(half):
            out[p, 0:ROWS, :] = first[pl.ds(p, ROWS, stride=half), :]
            out[p, ROWS : 2 * ROWS, :] = second[pl.ds(p, ROWS, stride=half), :]

    @pl.when(g == 0)
    def _():
        put(keep, got)

    @pl.when(g == 1)
    def _():
        put(got, keep)


def steps(count, shift):
    return [(i, (i + shift) % count) for i in range(count)]


def on_device(estimate, views, shifts, kernels, coverage):
    strips = lax.axis_size("xy")
    count = 2 * strips
    half = PLANES // 2
    quart = (QFLAT, WIDTH)
    both = [kernels[0], kernels[0][:, ::-1]]
    taps = jnp.pad(jnp.concatenate(both, axis=0), ((0, 2), (0, WIDTH - kernels.shape[2])))

    eb, em, eo, vm, vo, mine, theirs = call(
        prep_kernel,
        [
            arr((half, 2 * ROWS, WIDTH), BF16),
            arr((half, ROWS, WIDTH), BF16),
            arr((half, ROWS, WIDTH), BF16),
            arr((half, ROWS, WIDTH), BF16),
            arr((half, ROWS, WIDTH), BF16),
            arr((half, QUARTER, WIDTH), F32),
            arr((half, QUARTER, WIDTH), F32),
        ],
    )(estimate, views)

    outward, inward = [], []
    for s in range(strips):
        outward += [(2 * s, 2 * ((s + 1) % strips)), (2 * s + 1, 2 * ((s - 1) % strips) + 1)]
        inward += [(2 * s, 2 * ((s - 1) % strips) + 1), (2 * s + 1, 2 * ((s + 1) % strips))]
    swap = steps(2, 1)
    e_far = [lax.ppermute(eo, STRIPS, outward), lax.ppermute(em, STRIPS, inward)]
    e_all = [eb, lax.ppermute(eb, "gz", swap)] + e_far
    v_far = [lax.ppermute(vo, STRIPS, outward), lax.ppermute(vm, STRIPS, inward)]
    v_all = [views[0], lax.ppermute(views[0], "gz", swap)] + v_far
    theirs = lax.ppermute(theirs, "gz", swap)
    every = [taps] + [lax.ppermute(taps, "view", steps(VIEWS, i)) for i in range(1, VIEWS)]

    yf, yb, zf, x1f, x2f, yd, zd, xd = call(
        own_mats_kernel,
        [
            arr((2 * ROWS, WIDTH), BF16),
            arr((2 * ROWS, WIDTH), BF16),
            arr((2 * PLANES, WIDTH), BF16),
            arr((2 * WIDTH, WIDTH), BF16),
            arr((WIDTH, WIDTH), BF16),
            arr((ROWS, WIDTH), BF16),
            arr((PLANES, WIDTH), BF16),
            arr((WIDTH, WIDTH), BF16),
        ],
        smem=(1,),
    )(taps, shifts)
    zb, x1b, x2b = call(
        all_mats_kernel,
        [
            arr((VIEWS, 2 * PLANES, WIDTH), BF16),
            arr((VIEWS, 2 * WIDTH, WIDTH), BF16),
            arr((VIEWS, WIDTH, WIDTH), BF16),
        ],
    )(*every)

    window = pltpu.VMEM((PLANES, SPAN, WIDTH), BF16)
    wide = pltpu.VMEM((SPAN * PLANES, WIDTH), F32)
    flat = pltpu.VMEM((FLAT, WIDTH), F32)
    pairs = pltpu.VMEM((QFLAT, 2 * WIDTH), BF16)
    total = pltpu.VMEM(quart, F32)

    pred = call(first_pred_kernel, arr((FLAT, WIDTH), F32), [window, flat, pairs])(
        *e_all, yf, zf, x1f, x2f
    )
    data, ratio = call(
        first_ratio_kernel, [arr((FLAT, WIDTH), BF16)] * 2, [window, flat, pairs]
    )(*v_all, yd, zd, xd, pred)

    def neighbours(x):
        return lax.ppermute(x, STRIPS, steps(count, 1)), lax.ppermute(x, STRIPS, steps(count, -1))

    field = None
    for step in range(ITERS):
        low, high = neighbours(ratio)
        parts = call(back_y_kernel, [arr(quart, BF16)] * VIEWS, [wide, flat])(low, ratio, high, yb)
        terms = [parts[0]] + [
            lax.ppermute(parts[i], "view", steps(VIEWS, i)) for i in range(1, VIEWS)
        ]
        if step == 0:
            field, sent = call(
                first_update_kernel,
                [arr(quart, F32), arr(quart, BF16)],
                [pairs, total, total],
                smem=(4,),
            )(
                *terms,
                coverage,
                mine.reshape(QFLAT // 2, WIDTH),
                theirs.reshape(QFLAT // 2, WIDTH),
                zb,
                x1b,
                x2b,
            )
            own = jnp.concatenate(
                [sent] + [lax.ppermute(sent, "view", steps(VIEWS, i)) for i in range(1, VIEWS)],
                axis=0,
            )
            low, high = neighbours(own)
            ratio = call(next_ratio_kernel, arr((FLAT, WIDTH), BF16), [wide, flat, pairs])(
                low, own, high, yf, zf, x1f, x2f, data
            )
        else:
            field = call(last_update_kernel, arr(quart, F32), [pairs, total], smem=(4,))(
                *terms, coverage, field, zb, x1b, x2b
            )
    pieces = [field] + [lax.ppermute(field, "view", steps(VIEWS, i)) for i in range(1, VIEWS)]
    keep, give = call(halves_kernel, [arr((ROWS * half, WIDTH), F32)] * 2)(*pieces)
    got = lax.ppermute(give, "gz", swap)
    return call(final_kernel, arr((half, 2 * ROWS, WIDTH), F32))(keep, got)


def solution(mesh):
    placed = (
        P("gz", "xy", None),
        P("view", "gz", "xy", None),
        P("view", None),
        P("view", None, None),
        P(),
    )
    return jax.shard_map(
        on_device, mesh=mesh, in_specs=placed, out_specs=P("gz", "xy", None), check_vma=False
    )
```

```python
import jax
import jax.numpy as jnp
from jax import lax
from jax.experimental import pallas as pl
from jax.experimental.pallas import tpu as pltpu
from jax.sharding import PartitionSpec as P

F32 = jnp.float32
BF16 = jnp.bfloat16
ITERS = 2
VIEWS = 4
PLANES = 64
ROWS = 32
WIDTH = 128
SPAN = 3 * ROWS
QUARTER = ROWS // VIEWS
FLAT = ROWS * PLANES
QFLAT = QUARTER * PLANES
HALF = 31
SHIFT = 32
CHUNK = 512
BLOCK = 128
STRIPS = ("xy", "gz")


def dot(a, b):
    return jnp.dot(a, b, preferred_element_type=F32)


def split(x):
    high = x.astype(BF16)
    return high, (x - high.astype(F32)).astype(BF16)


def call(kernel, outs, scratch=(), flops=10**8, smem=()):
    def run(*args):
        n = len(args)
        specs = [
            pl.BlockSpec(memory_space=pltpu.SMEM if i in smem else pltpu.VMEM) for i in range(n)
        ]
        one = not isinstance(outs, (list, tuple))
        shapes = [outs] if one else list(outs)
        made = pl.pallas_call(
            kernel,
            out_shape=shapes,
            in_specs=specs,
            out_specs=[pl.BlockSpec(memory_space=pltpu.VMEM)] * len(shapes),
            scratch_shapes=list(scratch),
            compiler_params=pltpu.CompilerParams(vmem_limit_bytes=16 << 20),
            cost_estimate=pl.CostEstimate(flops=flops, bytes_accessed=4 << 20, transcendentals=0),
        )(*args)
        return made[0] if one else made

    return run


def arr(shape, dtype):
    return jax.ShapeDtypeStruct(shape, dtype)


def strip_index():
    return lax.axis_index("xy") * 2 + lax.axis_index("gz")


def prep_estimate_kernel(est, eb, em, eo, mine, theirs):
    v, g = lax.axis_index("view"), lax.axis_index("gz")
    eb[...] = est[...].astype(BF16)

    @pl.when(g == 0)
    def _():
        em[...] = est[:, 0:ROWS, :].astype(BF16)
        eo[...] = est[:, ROWS : 2 * ROWS, :].astype(BF16)

    @pl.when(g == 1)
    def _():
        eo[...] = est[:, 0:ROWS, :].astype(BF16)
        em[...] = est[:, ROWS : 2 * ROWS, :].astype(BF16)

    here = pl.multiple_of(g * ROWS + v * QUARTER, QUARTER)
    there = pl.multiple_of((1 - g) * ROWS + v * QUARTER, QUARTER)
    mine[...] = est[:, pl.ds(here, QUARTER), :]
    theirs[...] = est[:, pl.ds(there, QUARTER), :]


def prep_views_kernel(views, vm, vo):
    g = lax.axis_index("gz")

    @pl.when(g == 0)
    def _():
        vm[...] = views[0, :, 0:ROWS, :]
        vo[...] = views[0, :, ROWS : 2 * ROWS, :]

    @pl.when(g == 1)
    def _():
        vo[...] = views[0, :, 0:ROWS, :]
        vm[...] = views[0, :, ROWS : 2 * ROWS, :]


def toeplitz(row, rows, shift):
    return pltpu.roll(jnp.broadcast_to(row, (rows, WIDTH)), shift, 1, stride=1, stride_axis=0)


def normed(taps):
    return taps / jnp.sum(taps, axis=1, keepdims=True)


def x_matrix(row):
    i = lax.broadcasted_iota(jnp.int32, (WIDTH, WIDTH), 0)
    j = lax.broadcasted_iota(jnp.int32, (WIDTH, WIDTH), 1)
    full = toeplitz(row, WIDTH, WIDTH - HALF)
    return jnp.where(jnp.abs(i - j) <= HALF, full, 0.0)


def row_valid(rows):
    r = strip_index()
    j = lax.broadcasted_iota(jnp.int32, (rows, WIDTH), 1)
    low = jnp.where(r == 0, ROWS, 0)
    high = jnp.where(r == 2 * lax.axis_size("xy") - 1, 2 * ROWS, SPAN)
    return (j >= low) & (j < high)


def own_mats_kernel(taps, shifts, yf, yb, zf, x1f, x2f, yd, xd):
    k = normed(taps[...])
    valid = row_valid(ROWS)
    for ref, row in ((yf, 1), (yb, 4)):
        h, l = split(jnp.where(valid, toeplitz(k[row : row + 1], ROWS, 1), 0.0))
        ref[0:ROWS, :] = h
        ref[ROWS : 2 * ROWS, :] = l
    lane = lax.broadcasted_iota(jnp.int32, (PLANES, WIDTH), 1)
    z = jnp.where(lane < PLANES, toeplitz(k[0:1], PLANES, WIDTH - HALF), 0.0)
    zh = z.astype(BF16).astype(F32)
    zf[0:PLANES, :] = (zh + pltpu.roll(zh, PLANES, 1)).astype(BF16)
    zf[PLANES : 2 * PLANES, :] = (z - zh).astype(BF16)
    h, l = split(x_matrix(k[5:6]))
    x1f[0:WIDTH, :] = h
    x1f[WIDTH : 2 * WIDTH, :] = h
    x2f[...] = l

    def hot(rows, offset):
        i = lax.broadcasted_iota(jnp.int32, (rows, WIDTH), 0)
        j = lax.broadcasted_iota(jnp.int32, (rows, WIDTH), 1)
        return jnp.where(j - i == offset, 1.0, 0.0)

    yd[...] = jnp.where(valid, hot(ROWS, shifts[0, 1] + ROWS), 0.0).astype(BF16)
    xd[...] = hot(WIDTH, -shifts[0, 2]).astype(BF16)


def all_mats_kernel(t0, t1, t2, t3, zb, x1b, x2b):
    for i, taps in enumerate((t0, t1, t2, t3)):
        k = normed(taps[...])
        zh, zl = split(toeplitz(k[3:4], PLANES, WIDTH - HALF))
        zb[i, 0:PLANES, :] = zh
        zb[i, PLANES : 2 * PLANES, :] = zl
        h, l = split(x_matrix(k[2:3]))
        x1b[i, 0:WIDTH, :] = h
        x1b[i, WIDTH : 2 * WIDTH, :] = h
        x2b[i] = l


def y_stage(pair, matrix, put):
    def body(c, carry):
        for u in range(8):
            p = c * 16 + 2 * u
            put(p, dot(matrix, pair(p)))
        return carry

    lax.fori_loop(0, PLANES // 16, body, 0)


def filtered_rows(t):
    def put(p, o):
        o = o[0:ROWS] + o[ROWS : 2 * ROWS]
        t[pl.ds(p * ROWS, ROWS), :] = o[:, 0:WIDTH]
        t[pl.ds(p * ROWS + ROWS, ROWS), :] = o[:, WIDTH : 2 * WIDTH]

    return put


def z_stage(t, zf):
    def body(c, carry):
        for u in range(4):
            r = c * 8 + 2 * u
            first, second = pl.ds(r, PLANES, stride=ROWS), pl.ds(r + 1, PLANES, stride=ROWS)
            h0, l0 = split(t[first, :])
            h1, l1 = split(t[second, :])
            rhs = jnp.concatenate(
                [jnp.concatenate([h0, h1], axis=1), jnp.concatenate([l0, l1], axis=1)], axis=0
            )
            o = dot(zf, rhs)
            o = o[0:PLANES] + o[PLANES : 2 * PLANES]
            t[first, :] = o[:, 0:WIDTH]
            t[second, :] = o[:, WIDTH : 2 * WIDTH]
        return carry

    lax.fori_loop(0, ROWS // 8, body, 0)


def x_stage(t, x1, x2, emit):
    def body(c, carry):
        h, l = split(t[pl.ds(c * CHUNK, CHUNK), :])
        emit(c, dot(jnp.concatenate([h, l], axis=1), x1) + dot(h, x2))
        return carry

    lax.fori_loop(0, FLAT // CHUNK, body, 0)


def gather_first(f, slab, other, far_a, far_b):
    g = lax.axis_index("gz")
    low, high = slice(0, PLANES // 2), slice(PLANES // 2, PLANES)

    @pl.when(g == 0)
    def _():
        f[low, ROWS:SPAN, :] = slab[...]
        f[high, ROWS:SPAN, :] = other[...]
        f[low, 0:ROWS, :] = far_a[...]
        f[high, 0:ROWS, :] = far_b[...]

    @pl.when(g == 1)
    def _():
        f[high, 0 : 2 * ROWS, :] = slab[...]
        f[low, 0 : 2 * ROWS, :] = other[...]
        f[high, 2 * ROWS : SPAN, :] = far_a[...]
        f[low, 2 * ROWS : SPAN, :] = far_b[...]


def window_pair(f):
    return lambda p: jnp.concatenate([f[p], f[p + 1]], axis=1)


def strips_pair(low, own, high):
    def pair(p):
        sides = [jnp.concatenate([ref[p], ref[p + 1]], axis=1) for ref in (low, own, high)]
        return jnp.concatenate(sides, axis=0)

    return pair


def chunk_planes(c):
    return pl.ds(c * (CHUNK // ROWS), CHUNK // ROWS)


def as_planes(x):
    return x.reshape(CHUNK // ROWS, ROWS, WIDTH)


def first_pred_kernel(slab, other, far_a, far_b, yf, zf, x1, x2, pred, f, t):
    gather_first(f, slab, other, far_a, far_b)
    y_stage(window_pair(f), yf[:, 0:SPAN], filtered_rows(t))
    z_stage(t, zf[...])

    def emit(c, x):
        pred[pl.ds(c * CHUNK, CHUNK), :] = x

    x_stage(t, x1[...], x2[...], emit)


def first_ratio_kernel(slab, other, far_a, far_b, yd, xd, shifts, pred, data, ratio, f, d):
    gather_first(f, slab, other, far_a, far_b)
    d[SHIFT : SHIFT + PLANES] = jnp.zeros((PLANES, ROWS, WIDTH), BF16)
    up = SHIFT - shifts[0, 0]

    def put(p, o):
        o = o.astype(BF16)
        d[p + up] = o[:, 0:WIDTH]
        d[p + 1 + up] = o[:, WIDTH : 2 * WIDTH]

    y_stage(window_pair(f), yd[:, 0:SPAN], put)

    def body(c, carry):
        moved = d[pl.ds(SHIFT + c * (CHUNK // ROWS), CHUNK // ROWS)]
        got = dot(moved.reshape(CHUNK, WIDTH), xd[...])
        data[chunk_planes(c)] = as_planes(got).astype(BF16)
        quot = got / (pred[pl.ds(c * CHUNK, CHUNK), :] + 0.05)
        ratio[chunk_planes(c)] = as_planes(quot).astype(BF16)
        return carry

    lax.fori_loop(0, FLAT // CHUNK, body, 0)


def back_y_kernel(low, own, high, yb, _, o0, o1, o2, o3, t):
    y_stage(strips_pair(low, own, high), yb[:, 0:SPAN], filtered_rows(t))
    v = lax.axis_index("view")
    for i, out in enumerate((o0, o1, o2, o3)):
        q = lax.rem(v + i, VIEWS) * QUARTER
        for r in range(QUARTER):
            out[r * PLANES : (r + 1) * PLANES, :] = t[
                pl.ds(q + r, PLANES, stride=ROWS), :
            ].astype(BF16)


def compose_kernel(p0, p1, p2, p3, own, c):
    v = lax.axis_index("view")
    for j, ref in enumerate((p0, p1, p2, p3)):
        q = pl.multiple_of(lax.rem(v - j + VIEWS, VIEWS) * QUARTER, QUARTER)
        c[:, pl.ds(q, QUARTER), :] = ref[...].astype(F32)
    own[...] = c[...].astype(BF16)


def next_ratio_kernel(low, own, high, yf, zf, x1, x2, data, ratio, t):
    y_stage(strips_pair(low, own, high), yf[:, 0:SPAN], filtered_rows(t))
    z_stage(t, zf[...])

    def emit(c, x):
        quot = as_planes(x + 0.05)
        ratio[chunk_planes(c)] = (data[chunk_planes(c)].astype(F32) / quot).astype(BF16)

    x_stage(t, x1[...], x2[...], emit)


def weighted_total(terms, coverage, zb, x1b, x2b, hl, acc):
    v = lax.axis_index("view")
    block = strip_index() * ROWS // BLOCK
    count = coverage[0, block, 0]
    for w in range(1, VIEWS):
        count = count + coverage[w, block, 0]
    for i, term in enumerate(terms):
        weight = coverage[lax.rem(v - i + VIEWS, VIEWS), block, 0].astype(F32)
        zmat = zb[i, :, 0:PLANES]
        for u in range(QUARTER // 2):
            at = 2 * u * PLANES
            rhs = jnp.concatenate(
                [term[at : at + PLANES, :], term[at + PLANES : at + 2 * PLANES, :]], axis=1
            )
            o = dot(zmat, rhs)
            zh, zl = split(o[0:PLANES] + o[PLANES : 2 * PLANES])
            hl[at : at + PLANES, 0:WIDTH] = zh[:, 0:WIDTH]
            hl[at : at + PLANES, WIDTH : 2 * WIDTH] = zl[:, 0:WIDTH]
            at = at + PLANES
            hl[at : at + PLANES, 0:WIDTH] = zh[:, WIDTH : 2 * WIDTH]
            hl[at : at + PLANES, WIDTH : 2 * WIDTH] = zl[:, WIDTH : 2 * WIDTH]
        got = weight * (dot(hl[...], x1b[i]) + dot(hl[:, 0:WIDTH], x2b[i]))
        acc[...] = got if i == 0 else acc[...] + got
    return count.astype(F32)


def updated(old, acc, count, new):
    for r in range(QUARTER):
        at = pl.ds(r, PLANES, stride=QUARTER)
        new[at, :] = old[at, :] * acc[r * PLANES : (r + 1) * PLANES, :] / count


def first_update_kernel(
    t0, t1, t2, t3, coverage, mine, theirs, zb, x1b, x2b, field, sent, hl, acc, fq
):
    g = lax.axis_index("gz")
    half = QFLAT // 2

    @pl.when(g == 0)
    def _():
        fq[0:half, :] = mine[...]
        fq[half:QFLAT, :] = theirs[...]

    @pl.when(g == 1)
    def _():
        fq[half:QFLAT, :] = mine[...]
        fq[0:half, :] = theirs[...]

    count = weighted_total((t0, t1, t2, t3), coverage, zb, x1b, x2b, hl, acc)
    updated(fq, acc, count, field)
    sent[...] = field[...].reshape(PLANES, QUARTER, WIDTH).astype(BF16)


def last_update_kernel(t0, t1, t2, t3, coverage, old, zb, x1b, x2b, keep, give, hl, acc, new):
    count = weighted_total((t0, t1, t2, t3), coverage, zb, x1b, x2b, hl, acc)
    updated(old, acc, count, new)
    g = lax.axis_index("gz")
    half = QFLAT // 2
    keep[...] = new[pl.ds(pl.multiple_of(g * half, half), half), :]
    give[...] = new[pl.ds(pl.multiple_of((1 - g) * half, half), half), :]


def final_kernel(k0, k1, k2, k3, g0, g1, g2, g3, out):
    v, g = lax.axis_index("view"), lax.axis_index("gz")
    for j, (ours, others) in enumerate(((k0, g0), (k1, g1), (k2, g2), (k3, g3))):
        q = lax.rem(v - j + VIEWS, VIEWS) * QUARTER
        here = pl.multiple_of(g * ROWS + q, QUARTER)
        there = pl.multiple_of((1 - g) * ROWS + q, QUARTER)
        shape = (PLANES // 2, QUARTER, WIDTH)
        out[:, pl.ds(here, QUARTER), :] = ours[...].reshape(shape)
        out[:, pl.ds(there, QUARTER), :] = others[...].reshape(shape)


def steps(count, shift):
    return [(i, (i + shift) % count) for i in range(count)]


def on_device(estimate, views, shifts, kernels, coverage):
    strips = lax.axis_size("xy")
    count = 2 * strips
    half = PLANES // 2
    quart = (QFLAT, WIDTH)
    strip = arr((PLANES, ROWS, WIDTH), BF16)
    both = [kernels[0], kernels[0][:, ::-1]]
    taps = jnp.pad(jnp.concatenate(both, axis=0), ((0, 2), (0, WIDTH - kernels.shape[2])))

    piece = arr((half, ROWS, WIDTH), BF16)
    eighth = arr((half, QUARTER, WIDTH), F32)
    eb, em, eo, mine, theirs = call(
        prep_estimate_kernel,
        [arr((half, 2 * ROWS, WIDTH), BF16), piece, piece, eighth, eighth],
    )(estimate)
    vm, vo = call(prep_views_kernel, [piece, piece])(views)

    outward, inward = [], []
    for s in range(strips):
        outward += [(2 * s, 2 * ((s + 1) % strips)), (2 * s + 1, 2 * ((s - 1) % strips) + 1)]
        inward += [(2 * s, 2 * ((s - 1) % strips) + 1), (2 * s + 1, 2 * ((s + 1) % strips))]
    swap = steps(2, 1)
    e_far = [lax.ppermute(eo, STRIPS, outward), lax.ppermute(em, STRIPS, inward)]
    e_all = [eb, lax.ppermute(eb, "gz", swap)] + e_far
    v_far = [lax.ppermute(vo, STRIPS, outward), lax.ppermute(vm, STRIPS, inward)]
    v_all = [views[0], lax.ppermute(views[0], "gz", swap)] + v_far

    yf, yb, zf, x1f, x2f, yd, xd = call(
        own_mats_kernel,
        [
            arr((2 * ROWS, WIDTH), BF16),
            arr((2 * ROWS, WIDTH), BF16),
            arr((2 * PLANES, WIDTH), BF16),
            arr((2 * WIDTH, WIDTH), BF16),
            arr((WIDTH, WIDTH), BF16),
            arr((ROWS, WIDTH), BF16),
            arr((WIDTH, WIDTH), BF16),
        ],
        smem=(1,),
    )(taps, shifts)

    window = pltpu.VMEM((PLANES, SPAN, WIDTH), BF16)
    shifted = pltpu.VMEM((PLANES + 2 * SHIFT, ROWS, WIDTH), BF16)
    flat = pltpu.VMEM((FLAT, WIDTH), F32)
    cube = pltpu.VMEM((PLANES, ROWS, WIDTH), F32)
    pairs = pltpu.VMEM((QFLAT, 2 * WIDTH), BF16)
    total = pltpu.VMEM(quart, F32)

    pred = call(first_pred_kernel, arr((FLAT, WIDTH), F32), [window, flat])(
        *e_all, yf, zf, x1f, x2f
    )
    data, ratio = call(first_ratio_kernel, [strip, strip], [window, shifted], smem=(6,))(
        *v_all, yd, xd, shifts, pred
    )

    def neighbours(x):
        return lax.ppermute(x, STRIPS, steps(count, 1)), lax.ppermute(x, STRIPS, steps(count, -1))

    def from_views(x):
        return [x] + [lax.ppermute(x, "view", steps(VIEWS, i)) for i in range(1, VIEWS)]

    late, theirs, _ = lax.optimization_barrier((taps, theirs, ratio))
    theirs = lax.ppermute(theirs, "gz", swap)
    zb, x1b, x2b = call(
        all_mats_kernel,
        [
            arr((VIEWS, 2 * PLANES, WIDTH), BF16),
            arr((VIEWS, 2 * WIDTH, WIDTH), BF16),
            arr((VIEWS, WIDTH, WIDTH), BF16),
        ],
    )(*from_views(late))

    field = None
    for step in range(ITERS):
        low, high = neighbours(ratio)
        parts = call(back_y_kernel, [arr(quart, BF16)] * VIEWS, [flat])(low, ratio, high, yb, zb)
        terms = [parts[0]] + [
            lax.ppermute(parts[i], "view", steps(VIEWS, i)) for i in range(1, VIEWS)
        ]
        if step == 0:
            field, sent = call(
                first_update_kernel,
                [arr(quart, F32), arr((PLANES, QUARTER, WIDTH), BF16)],
                [pairs, total, total],
                smem=(4,),
            )(
                *terms,
                coverage,
                mine.reshape(QFLAT // 2, WIDTH),
                theirs.reshape(QFLAT // 2, WIDTH),
                zb,
                x1b,
                x2b,
            )
            own = call(compose_kernel, strip, [cube])(*from_views(sent))
            low, high = neighbours(own)
            ratio = call(next_ratio_kernel, strip, [flat])(
                low, own, high, yf, zf, x1f, x2f, data
            )
        else:
            keep, give = call(
                last_update_kernel,
                [arr((QFLAT // 2, WIDTH), F32)] * 2,
                [pairs, total, total],
                smem=(4,),
            )(*terms, coverage, field, zb, x1b, x2b)
    got = lax.ppermute(give, "gz", swap)
    return call(final_kernel, arr((half, 2 * ROWS, WIDTH), F32))(
        *from_views(keep), *from_views(got)
    )


def solution(mesh):
    placed = (
        P("gz", "xy", None),
        P("view", "gz", "xy", None),
        P("view", None),
        P("view", None, None),
        P(),
    )
    return jax.shard_map(
        on_device, mesh=mesh, in_specs=placed, out_specs=P("gz", "xy", None), check_vma=False
    )
```

```python
import jax
import jax.numpy as jnp
from jax import lax
from jax.experimental import pallas as pl
from jax.experimental.pallas import tpu as pltpu
from jax.sharding import PartitionSpec as P

F32 = jnp.float32
BF16 = jnp.bfloat16
ITERS = 2
VIEWS = 4
PLANES = 64
ROWS = 32
WIDTH = 128
SPAN = 3 * ROWS
QUARTER = ROWS // VIEWS
FLAT = ROWS * PLANES
QFLAT = QUARTER * PLANES
HALF = 31
SHIFT = 32
CHUNK = 512
BLOCK = 128
STRIPS = ("xy", "gz")


def dot(a, b):
    return jnp.dot(a, b, preferred_element_type=F32)


def split(x):
    high = x.astype(BF16)
    return high, (x - high.astype(F32)).astype(BF16)


def call(kernel, outs, scratch=(), flops=10**8, smem=()):
    def run(*args):
        n = len(args)
        specs = [
            pl.BlockSpec(memory_space=pltpu.SMEM if i in smem else pltpu.VMEM) for i in range(n)
        ]
        one = not isinstance(outs, (list, tuple))
        shapes = [outs] if one else list(outs)
        made = pl.pallas_call(
            kernel,
            out_shape=shapes,
            in_specs=specs,
            out_specs=[pl.BlockSpec(memory_space=pltpu.VMEM)] * len(shapes),
            scratch_shapes=list(scratch),
            compiler_params=pltpu.CompilerParams(vmem_limit_bytes=16 << 20),
            cost_estimate=pl.CostEstimate(flops=flops, bytes_accessed=4 << 20, transcendentals=0),
        )(*args)
        return made[0] if one else made

    return run


def loop(count, body):
    for c in range(count):
        body(c)


def arr(shape, dtype):
    return jax.ShapeDtypeStruct(shape, dtype)


def strip_index():
    return lax.axis_index("xy") * 2 + lax.axis_index("gz")


def prep_estimate_kernel(est, eb, em, eo, mine, theirs):
    v, g = lax.axis_index("view"), lax.axis_index("gz")
    eb[...] = est[...].astype(BF16)

    @pl.when(g == 0)
    def _():
        em[...] = est[:, 0:ROWS, :].astype(BF16)
        eo[...] = est[:, ROWS : 2 * ROWS, :].astype(BF16)

    @pl.when(g == 1)
    def _():
        eo[...] = est[:, 0:ROWS, :].astype(BF16)
        em[...] = est[:, ROWS : 2 * ROWS, :].astype(BF16)

    here = pl.multiple_of(g * ROWS + v * QUARTER, QUARTER)
    there = pl.multiple_of((1 - g) * ROWS + v * QUARTER, QUARTER)
    mine[...] = est[:, pl.ds(here, QUARTER), :]
    theirs[...] = est[:, pl.ds(there, QUARTER), :]


def prep_views_kernel(views, vm, vo):
    g = lax.axis_index("gz")

    @pl.when(g == 0)
    def _():
        vm[...] = views[0, :, 0:ROWS, :]
        vo[...] = views[0, :, ROWS : 2 * ROWS, :]

    @pl.when(g == 1)
    def _():
        vo[...] = views[0, :, 0:ROWS, :]
        vm[...] = views[0, :, ROWS : 2 * ROWS, :]


def toeplitz(row, rows, shift):
    return pltpu.roll(jnp.broadcast_to(row, (rows, WIDTH)), shift, 1, stride=1, stride_axis=0)


def normed(taps):
    return taps / jnp.sum(taps, axis=1, keepdims=True)


def x_matrix(row):
    i = lax.broadcasted_iota(jnp.int32, (WIDTH, WIDTH), 0)
    j = lax.broadcasted_iota(jnp.int32, (WIDTH, WIDTH), 1)
    full = toeplitz(row, WIDTH, WIDTH - HALF)
    return jnp.where(jnp.abs(i - j) <= HALF, full, 0.0)


def row_valid(rows):
    r = strip_index()
    j = lax.broadcasted_iota(jnp.int32, (rows, WIDTH), 1)
    low = jnp.where(r == 0, ROWS, 0)
    high = jnp.where(r == 2 * lax.axis_size("xy") - 1, 2 * ROWS, SPAN)
    return (j >= low) & (j < high)


def own_mats_kernel(taps, shifts, yw, yf, yb, zf, x1f, x2f, yd, xd):
    k = normed(taps[...])
    valid = row_valid(ROWS)
    column = lax.broadcasted_iota(jnp.int32, (ROWS, WIDTH), 1)
    kept = (lax.axis_index("gz") == 0) | ((column >= ROWS) & (column < 2 * ROWS))

    def sides(y):
        return jnp.where(kept, y, pltpu.roll(y, 2 * ROWS, 1))

    forward = jnp.where(valid, toeplitz(k[1:2], ROWS, 1), 0.0)
    backward = jnp.where(valid, toeplitz(k[4:5], ROWS, 1), 0.0)
    for ref, y in ((yw, forward), (yf, sides(forward)), (yb, sides(backward))):
        h, l = split(y)
        ref[0:ROWS, :] = h
        ref[ROWS : 2 * ROWS, :] = l
    lane = lax.broadcasted_iota(jnp.int32, (PLANES, WIDTH), 1)
    z = jnp.where(lane < PLANES, toeplitz(k[0:1], PLANES, WIDTH - HALF), 0.0)
    zh = z.astype(BF16).astype(F32)
    zf[0:PLANES, :] = (zh + pltpu.roll(zh, PLANES, 1)).astype(BF16)
    zf[PLANES : 2 * PLANES, :] = (z - zh).astype(BF16)
    h, l = split(x_matrix(k[5:6]))
    x1f[0:WIDTH, :] = h
    x1f[WIDTH : 2 * WIDTH, :] = h
    x2f[...] = l

    def hot(rows, offset):
        i = lax.broadcasted_iota(jnp.int32, (rows, WIDTH), 0)
        j = lax.broadcasted_iota(jnp.int32, (rows, WIDTH), 1)
        return jnp.where(j - i == offset, 1.0, 0.0)

    yd[...] = jnp.where(valid, hot(ROWS, shifts[0, 1] + ROWS), 0.0).astype(BF16)
    xd[...] = hot(WIDTH, -shifts[0, 2]).astype(BF16)


def all_mats_kernel(t0, t1, t2, t3, zb, x1b, x2b):
    for i, taps in enumerate((t0, t1, t2, t3)):
        k = normed(taps[...])
        zh, zl = split(toeplitz(k[3:4], PLANES, WIDTH - HALF))
        zb[i, 0:PLANES, :] = zh
        zb[i, PLANES : 2 * PLANES, :] = zl
        h, l = split(x_matrix(k[2:3]))
        x1b[i, 0:WIDTH, :] = h
        x1b[i, WIDTH : 2 * WIDTH, :] = h
        x2b[i] = l


def y_stage(pair, matrix, put):
    loop(PLANES // 2, lambda c: put(2 * c, dot(matrix, pair(2 * c))))


def filtered_rows(t):
    def put(p, o):
        o = o[0:ROWS] + o[ROWS : 2 * ROWS]
        t[pl.ds(p * ROWS, ROWS), :] = o[:, 0:WIDTH]
        t[pl.ds(p * ROWS + ROWS, ROWS), :] = o[:, WIDTH : 2 * WIDTH]

    return put


def z_stage(t, u, zf):
    def body(c):
        first, second = (pl.ds(2 * c + k, PLANES, stride=ROWS) for k in (0, 1))
        h0, l0 = split(t[first, :])
        h1, l1 = split(t[second, :])
        rhs = jnp.concatenate(
            [jnp.concatenate([h0, h1], axis=1), jnp.concatenate([l0, l1], axis=1)], axis=0
        )
        o = dot(zf, rhs)
        o = o[0:PLANES] + o[PLANES : 2 * PLANES]
        u[first, :] = o[:, 0:WIDTH]
        u[second, :] = o[:, WIDTH : 2 * WIDTH]

    loop(ROWS // 2, body)


def x_stage(t, x1, x2, emit):
    def body(c):
        h, l = split(t[pl.ds(c * CHUNK, CHUNK), :])
        emit(c, dot(jnp.concatenate([h, l], axis=1), x1) + dot(h, x2))

    loop(FLAT // CHUNK, body)


def gather_first(f, slab, other, far_a, far_b):
    g = lax.axis_index("gz")
    low, high = slice(0, PLANES // 2), slice(PLANES // 2, PLANES)

    @pl.when(g == 0)
    def _():
        f[low, ROWS:SPAN, :] = slab[...]
        f[high, ROWS:SPAN, :] = other[...]
        f[low, 0:ROWS, :] = far_a[...]
        f[high, 0:ROWS, :] = far_b[...]

    @pl.when(g == 1)
    def _():
        f[high, 0 : 2 * ROWS, :] = slab[...]
        f[low, 0 : 2 * ROWS, :] = other[...]
        f[high, 2 * ROWS : SPAN, :] = far_a[...]
        f[low, 2 * ROWS : SPAN, :] = far_b[...]


def window_pair(f):
    return lambda p: jnp.concatenate([f[p], f[p + 1]], axis=1)


def strips_pair(far, own, near):
    def pair(p):
        sides = [jnp.concatenate([ref[p], ref[p + 1]], axis=1) for ref in (far, own, near)]
        return jnp.concatenate(sides, axis=0)

    return pair


def chunk_planes(c):
    return pl.ds(c * (CHUNK // ROWS), CHUNK // ROWS)


def as_planes(x):
    return x.reshape(CHUNK // ROWS, ROWS, WIDTH)


def first_pred_kernel(slab, other, far_a, far_b, yw, zf, x1, x2, pred, f, t, u):
    gather_first(f, slab, other, far_a, far_b)
    y_stage(window_pair(f), yw[:, 0:SPAN], filtered_rows(t))
    z_stage(t, u, zf[...])

    def emit(c, x):
        pred[pl.ds(c * CHUNK, CHUNK), :] = x

    x_stage(u, x1[...], x2[...], emit)


def first_ratio_kernel(slab, other, far_a, far_b, yd, xd, shifts, pred, data, ratio, f, d):
    gather_first(f, slab, other, far_a, far_b)
    d[SHIFT : SHIFT + PLANES] = jnp.zeros((PLANES, ROWS, WIDTH), BF16)
    up = SHIFT - shifts[0, 0]

    def put(p, o):
        o = o.astype(BF16)
        d[p + up] = o[:, 0:WIDTH]
        d[p + 1 + up] = o[:, WIDTH : 2 * WIDTH]

    y_stage(window_pair(f), yd[:, 0:SPAN], put)

    def body(c):
        moved = d[pl.ds(SHIFT + c * (CHUNK // ROWS), CHUNK // ROWS)]
        got = dot(moved.reshape(CHUNK, WIDTH), xd[...])
        data[chunk_planes(c)] = as_planes(got).astype(BF16)
        quot = got / (pred[pl.ds(c * CHUNK, CHUNK), :] + 0.05)
        ratio[chunk_planes(c)] = as_planes(quot).astype(BF16)

    loop(FLAT // CHUNK, body)


def back_y_kernel(far, own, near, yb, _, o0, o1, o2, o3, t):
    y_stage(strips_pair(far, own, near), yb[:, 0:SPAN], filtered_rows(t))
    v = lax.axis_index("view")
    for i, out in enumerate((o0, o1, o2, o3)):
        q = lax.rem(v + i, VIEWS) * QUARTER
        for r in range(QUARTER):
            out[r * PLANES : (r + 1) * PLANES, :] = t[
                pl.ds(q + r, PLANES, stride=ROWS), :
            ].astype(BF16)


def compose_kernel(p0, p1, p2, p3, own, c):
    v = lax.axis_index("view")
    for j, ref in enumerate((p0, p1, p2, p3)):
        q = pl.multiple_of(lax.rem(v - j + VIEWS, VIEWS) * QUARTER, QUARTER)
        c[:, pl.ds(q, QUARTER), :] = ref[...].astype(F32)
    own[...] = c[...].astype(BF16)


def next_ratio_kernel(far, own, near, yf, zf, x1, x2, data, ratio, t, u):
    y_stage(strips_pair(far, own, near), yf[:, 0:SPAN], filtered_rows(t))
    z_stage(t, u, zf[...])

    def emit(c, x):
        quot = as_planes(x + 0.05)
        ratio[chunk_planes(c)] = (data[chunk_planes(c)].astype(F32) / quot).astype(BF16)

    x_stage(u, x1[...], x2[...], emit)


def weighted_total(terms, coverage, zb, x1b, x2b, hl, acc):
    v = lax.axis_index("view")
    block = strip_index() * ROWS // BLOCK
    count = coverage[0, block, 0]
    for w in range(1, VIEWS):
        count = count + coverage[w, block, 0]
    for i, term in enumerate(terms):
        weight = coverage[lax.rem(v - i + VIEWS, VIEWS), block, 0].astype(F32)
        zmat = zb[i, :, 0:PLANES]
        for u in range(QUARTER // 2):
            at = 2 * u * PLANES
            rhs = jnp.concatenate(
                [term[at : at + PLANES, :], term[at + PLANES : at + 2 * PLANES, :]], axis=1
            )
            o = dot(zmat, rhs)
            zh, zl = split(o[0:PLANES] + o[PLANES : 2 * PLANES])
            hl[at : at + PLANES, 0:WIDTH] = zh[:, 0:WIDTH]
            hl[at : at + PLANES, WIDTH : 2 * WIDTH] = zl[:, 0:WIDTH]
            at = at + PLANES
            hl[at : at + PLANES, 0:WIDTH] = zh[:, WIDTH : 2 * WIDTH]
            hl[at : at + PLANES, WIDTH : 2 * WIDTH] = zl[:, WIDTH : 2 * WIDTH]
        got = weight * (dot(hl[...], x1b[i]) + dot(hl[:, 0:WIDTH], x2b[i]))
        acc[...] = got if i == 0 else acc[...] + got
    return count.astype(F32)


def updated(old, acc, count, new):
    for r in range(QUARTER):
        at = pl.ds(r, PLANES, stride=QUARTER)
        new[at, :] = old[at, :] * acc[r * PLANES : (r + 1) * PLANES, :] / count


def first_update_kernel(
    t0, t1, t2, t3, coverage, mine, theirs, zb, x1b, x2b, field, sent, hl, acc, fq
):
    g = lax.axis_index("gz")
    half = QFLAT // 2

    @pl.when(g == 0)
    def _():
        fq[0:half, :] = mine[...]
        fq[half:QFLAT, :] = theirs[...]

    @pl.when(g == 1)
    def _():
        fq[half:QFLAT, :] = mine[...]
        fq[0:half, :] = theirs[...]

    count = weighted_total((t0, t1, t2, t3), coverage, zb, x1b, x2b, hl, acc)
    updated(fq, acc, count, field)
    sent[...] = field[...].reshape(PLANES, QUARTER, WIDTH).astype(BF16)


def last_update_kernel(t0, t1, t2, t3, coverage, old, zb, x1b, x2b, keep, give, hl, acc, new):
    count = weighted_total((t0, t1, t2, t3), coverage, zb, x1b, x2b, hl, acc)
    updated(old, acc, count, new)
    g = lax.axis_index("gz")
    half = QFLAT // 2
    keep[...] = new[pl.ds(pl.multiple_of(g * half, half), half), :]
    give[...] = new[pl.ds(pl.multiple_of((1 - g) * half, half), half), :]


def final_kernel(k0, k1, k2, k3, g0, g1, g2, g3, out):
    v, g = lax.axis_index("view"), lax.axis_index("gz")
    for j, (ours, others) in enumerate(((k0, g0), (k1, g1), (k2, g2), (k3, g3))):
        q = lax.rem(v - j + VIEWS, VIEWS) * QUARTER
        here = pl.multiple_of(g * ROWS + q, QUARTER)
        there = pl.multiple_of((1 - g) * ROWS + q, QUARTER)
        shape = (PLANES // 2, QUARTER, WIDTH)
        out[:, pl.ds(here, QUARTER), :] = ours[...].reshape(shape)
        out[:, pl.ds(there, QUARTER), :] = others[...].reshape(shape)


def steps(count, shift):
    return [(i, (i + shift) % count) for i in range(count)]


def on_device(estimate, views, shifts, kernels, coverage):
    strips = lax.axis_size("xy")
    count = 2 * strips
    half = PLANES // 2
    quart = (QFLAT, WIDTH)
    strip = arr((PLANES, ROWS, WIDTH), BF16)
    both = [kernels[0], kernels[0][:, ::-1]]
    taps = jnp.pad(jnp.concatenate(both, axis=0), ((0, 2), (0, WIDTH - kernels.shape[2])))

    piece = arr((half, ROWS, WIDTH), BF16)
    eighth = arr((half, QUARTER, WIDTH), F32)
    eb, em, eo, mine, theirs = call(
        prep_estimate_kernel,
        [arr((half, 2 * ROWS, WIDTH), BF16), piece, piece, eighth, eighth],
    )(estimate)
    vm, vo = call(prep_views_kernel, [piece, piece])(views)

    outward, inward = [], []
    for s in range(strips):
        outward += [(2 * s, 2 * ((s + 1) % strips)), (2 * s + 1, 2 * ((s - 1) % strips) + 1)]
        inward += [(2 * s, 2 * ((s - 1) % strips) + 1), (2 * s + 1, 2 * ((s + 1) % strips))]
    swap = steps(2, 1)
    e_far = [lax.ppermute(eo, STRIPS, outward), lax.ppermute(em, STRIPS, inward)]
    e_all = [eb, lax.ppermute(eb, "gz", swap)] + e_far
    v_far = [lax.ppermute(vo, STRIPS, outward), lax.ppermute(vm, STRIPS, inward)]
    v_all = [views[0], lax.ppermute(views[0], "gz", swap)] + v_far

    yw, yf, yb, zf, x1f, x2f, yd, xd = call(
        own_mats_kernel,
        [
            arr((2 * ROWS, WIDTH), BF16),
            arr((2 * ROWS, WIDTH), BF16),
            arr((2 * ROWS, WIDTH), BF16),
            arr((2 * PLANES, WIDTH), BF16),
            arr((2 * WIDTH, WIDTH), BF16),
            arr((WIDTH, WIDTH), BF16),
            arr((ROWS, WIDTH), BF16),
            arr((WIDTH, WIDTH), BF16),
        ],
        smem=(1,),
    )(taps, shifts)

    window = pltpu.VMEM((PLANES, SPAN, WIDTH), BF16)
    shifted = pltpu.VMEM((PLANES + 2 * SHIFT, ROWS, WIDTH), BF16)
    flat = pltpu.VMEM((FLAT, WIDTH), F32)
    cube = pltpu.VMEM((PLANES, ROWS, WIDTH), F32)
    pairs = pltpu.VMEM((QFLAT, 2 * WIDTH), BF16)
    total = pltpu.VMEM(quart, F32)

    pred = call(first_pred_kernel, arr((FLAT, WIDTH), F32), [window, flat, flat])(
        *e_all, yw, zf, x1f, x2f
    )
    data, ratio = call(first_ratio_kernel, [strip, strip], [window, shifted], smem=(6,))(
        *v_all, yd, xd, shifts, pred
    )

    across = [(i, (i + 1 if i % 2 else i - 1) % count) for i in range(count)]

    def neighbours(x):
        return lax.ppermute(x, STRIPS, across), lax.ppermute(x, "gz", swap)

    def from_views(x):
        return [x] + [lax.ppermute(x, "view", steps(VIEWS, i)) for i in range(1, VIEWS)]

    late, theirs, _ = lax.optimization_barrier((taps, theirs, ratio))
    theirs = lax.ppermute(theirs, "gz", swap)
    zb, x1b, x2b = call(
        all_mats_kernel,
        [
            arr((VIEWS, 2 * PLANES, WIDTH), BF16),
            arr((VIEWS, 2 * WIDTH, WIDTH), BF16),
            arr((VIEWS, WIDTH, WIDTH), BF16),
        ],
    )(*from_views(late))

    field = None
    for step in range(ITERS):
        far, near = neighbours(ratio)
        parts = call(back_y_kernel, [arr(quart, BF16)] * VIEWS, [flat])(far, ratio, near, yb, zb)
        terms = [parts[0]] + [
            lax.ppermute(parts[i], "view", steps(VIEWS, i)) for i in range(1, VIEWS)
        ]
        if step == 0:
            field, sent = call(
                first_update_kernel,
                [arr(quart, F32), arr((PLANES, QUARTER, WIDTH), BF16)],
                [pairs, total, total],
                smem=(4,),
            )(
                *terms,
                coverage,
                mine.reshape(QFLAT // 2, WIDTH),
                theirs.reshape(QFLAT // 2, WIDTH),
                zb,
                x1b,
                x2b,
            )
            own = call(compose_kernel, strip, [cube])(*from_views(sent))
            far, near = neighbours(own)
            ratio = call(next_ratio_kernel, strip, [flat, flat])(
                far, own, near, yf, zf, x1f, x2f, data
            )
        else:
            keep, give = call(
                last_update_kernel,
                [arr((QFLAT // 2, WIDTH), F32)] * 2,
                [pairs, total, total],
                smem=(4,),
            )(*terms, coverage, field, zb, x1b, x2b)
    got = lax.ppermute(give, "gz", swap)
    return call(final_kernel, arr((half, 2 * ROWS, WIDTH), F32))(
        *from_views(keep), *from_views(got)
    )


def solution(mesh):
    placed = (
        P("gz", "xy", None),
        P("view", "gz", "xy", None),
        P("view", None),
        P("view", None, None),
        P(),
    )
    return jax.shard_map(
        on_device, mesh=mesh, in_specs=placed, out_specs=P("gz", "xy", None), check_vma=False
    )
```

```python
import jax
import jax.numpy as jnp
from jax import lax
from jax.experimental import pallas as pl
from jax.experimental.pallas import tpu as pltpu
from jax.sharding import PartitionSpec as P

F32 = jnp.float32
BF16 = jnp.bfloat16
F16 = jnp.float16
ITERS = 2
VIEWS = 4
PLANES = 64
ROWS = 32
WIDTH = 128
SPAN = 3 * ROWS
QUARTER = ROWS // VIEWS
FLAT = ROWS * PLANES
QFLAT = QUARTER * PLANES
HALF = 31
SHIFT = 32
CHUNK = 512
TAIL = 8
BLOCK = 128
STRIPS = ("xy", "gz")


def dot(a, b):
    return jnp.dot(a, b, preferred_element_type=F32)


def split(x):
    high = x.astype(BF16)
    return high, (x - high.astype(F32)).astype(BF16)


def call(kernel, outs, scratch=(), flops=10**8, smem=()):
    def space(i):
        return pltpu.SMEM if i in smem else pltpu.VMEM

    def run(*args):
        specs = [pl.BlockSpec(memory_space=space(i)) for i in range(len(args))]
        one = not isinstance(outs, (list, tuple))
        shapes = [outs] if one else list(outs)
        made = pl.pallas_call(
            kernel,
            out_shape=shapes,
            in_specs=specs,
            out_specs=[pl.BlockSpec(memory_space=pltpu.VMEM)] * len(shapes),
            scratch_shapes=list(scratch),
            compiler_params=pltpu.CompilerParams(vmem_limit_bytes=16 << 20),
            cost_estimate=pl.CostEstimate(flops=flops, bytes_accessed=4 << 20, transcendentals=0),
        )(*args)
        return made[0] if one else made

    return run


def loop(count, body):
    for c in range(count):
        body(c)


def arr(shape, dtype):
    return jax.ShapeDtypeStruct(shape, dtype)


def strip_index():
    return lax.axis_index("xy") * 2 + lax.axis_index("gz")


def prep_estimate_kernel(est, eb, em, eo, mine, theirs):
    v, g = lax.axis_index("view"), lax.axis_index("gz")
    eb[...] = est[...].astype(BF16)

    @pl.when(g == 0)
    def _():
        em[...] = est[:, 0:ROWS, :].astype(BF16)
        eo[...] = est[:, ROWS : 2 * ROWS, :].astype(BF16)

    @pl.when(g == 1)
    def _():
        eo[...] = est[:, 0:ROWS, :].astype(BF16)
        em[...] = est[:, ROWS : 2 * ROWS, :].astype(BF16)

    here = pl.multiple_of(g * ROWS + v * QUARTER, QUARTER)
    there = pl.multiple_of((1 - g) * ROWS + v * QUARTER, QUARTER)
    mine[...] = est[:, pl.ds(here, QUARTER), :]
    theirs[...] = est[:, pl.ds(there, QUARTER), :]


def prep_views_kernel(views, vm, vo):
    g = lax.axis_index("gz")

    @pl.when(g == 0)
    def _():
        vm[...] = views[0, :, 0:ROWS, :]
        vo[...] = views[0, :, ROWS : 2 * ROWS, :]

    @pl.when(g == 1)
    def _():
        vo[...] = views[0, :, 0:ROWS, :]
        vm[...] = views[0, :, ROWS : 2 * ROWS, :]


def toeplitz(row, rows, shift):
    return pltpu.roll(jnp.broadcast_to(row, (rows, WIDTH)), shift, 1, stride=1, stride_axis=0)


def normed(taps):
    return taps / jnp.sum(taps, axis=1, keepdims=True)


def x_matrix(row):
    i = lax.broadcasted_iota(jnp.int32, (WIDTH, WIDTH), 0)
    j = lax.broadcasted_iota(jnp.int32, (WIDTH, WIDTH), 1)
    full = toeplitz(row, WIDTH, WIDTH - HALF)
    return jnp.where(jnp.abs(i - j) <= HALF, full, 0.0)


def row_valid(rows):
    r = strip_index()
    j = lax.broadcasted_iota(jnp.int32, (rows, WIDTH), 1)
    low = jnp.where(r == 0, ROWS, 0)
    high = jnp.where(r == 2 * lax.axis_size("xy") - 1, 2 * ROWS, SPAN)
    return (j >= low) & (j < high)


def own_mats_kernel(taps, shifts, yw, yf, yb, zf, x1f, x2f, yd, xd):
    k = normed(taps[...])
    valid = row_valid(ROWS)
    column = lax.broadcasted_iota(jnp.int32, (ROWS, WIDTH), 1)
    kept = (lax.axis_index("gz") == 0) | ((column >= ROWS) & (column < 2 * ROWS))

    def sides(y):
        return jnp.where(kept, y, pltpu.roll(y, 2 * ROWS, 1))

    forward = jnp.where(valid, toeplitz(k[1:2], ROWS, 1), 0.0)
    backward = jnp.where(valid, toeplitz(k[4:5], ROWS, 1), 0.0)
    for ref, y in ((yw, forward), (yf, sides(forward)), (yb, sides(backward))):
        h, l = split(y)
        ref[0:ROWS, :] = h
        ref[ROWS : 2 * ROWS, :] = l
    lane = lax.broadcasted_iota(jnp.int32, (PLANES, WIDTH), 1)
    z = jnp.where(lane < PLANES, toeplitz(k[0:1], PLANES, WIDTH - HALF), 0.0)
    zh = z.astype(BF16).astype(F32)
    zf[0:PLANES, :] = (zh + pltpu.roll(zh, PLANES, 1)).astype(BF16)
    zf[PLANES : 2 * PLANES, :] = (z - zh).astype(BF16)
    h, l = split(x_matrix(k[5:6]))
    x1f[0:WIDTH, :] = h
    x1f[WIDTH : 2 * WIDTH, :] = h
    x2f[...] = l

    def hot(rows, offset):
        i = lax.broadcasted_iota(jnp.int32, (rows, WIDTH), 0)
        j = lax.broadcasted_iota(jnp.int32, (rows, WIDTH), 1)
        return jnp.where(j - i == offset, 1.0, 0.0)

    yd[...] = jnp.where(valid, hot(ROWS, shifts[0, 1] + ROWS), 0.0).astype(BF16)
    xd[...] = hot(WIDTH, -shifts[0, 2]).astype(BF16)


def all_mats_kernel(t0, t1, t2, t3, coverage, zb, x1b, x2b):
    v = lax.axis_index("view")
    block = strip_index() * ROWS // BLOCK
    for i, taps in enumerate((t0, t1, t2, t3)):
        k = normed(taps[...])
        zh, zl = split(toeplitz(k[3:4], PLANES, WIDTH - HALF))
        zb[i, 0:PLANES, :] = zh
        zb[i, PLANES : 2 * PLANES, :] = zl
        weight = coverage[lax.rem(v - i + VIEWS, VIEWS), block, 0].astype(F32)
        h, l = split(weight * x_matrix(k[2:3]))
        at = slice(i * WIDTH, (i + 1) * WIDTH)
        x1b[at, :] = h
        x1b[VIEWS * WIDTH + i * WIDTH : VIEWS * WIDTH + (i + 1) * WIDTH, :] = h
        x2b[at, :] = l


def y_stage(pair, matrix, put):
    loop(PLANES // 2, lambda c: put(2 * c, dot(matrix, pair(2 * c))))


def filtered_rows(t):
    def put(p, o):
        o = o[0:ROWS] + o[ROWS : 2 * ROWS]
        t[pl.ds(p * ROWS, ROWS), :] = o[:, 0:WIDTH]
        t[pl.ds(p * ROWS + ROWS, ROWS), :] = o[:, WIDTH : 2 * WIDTH]

    return put


def z_stage(t, u, zf):
    def body(c):
        first, second = (pl.ds(2 * c + k, PLANES, stride=ROWS) for k in (0, 1))
        h0, l0 = split(t[first, :])
        h1, l1 = split(t[second, :])
        rhs = jnp.concatenate(
            [jnp.concatenate([h0, h1], axis=1), jnp.concatenate([l0, l1], axis=1)], axis=0
        )
        o = dot(zf, rhs)
        o = o[0:PLANES] + o[PLANES : 2 * PLANES]
        u[first, :] = o[:, 0:WIDTH]
        u[second, :] = o[:, WIDTH : 2 * WIDTH]

    loop(ROWS // 2, body)


def x_stage(t, x1, x2, emit):
    def body(c):
        h, l = split(t[pl.ds(c * CHUNK, CHUNK), :])
        emit(c, dot(jnp.concatenate([h, l], axis=1), x1) + dot(h, x2))

    loop(FLAT // CHUNK, body)


def gather_first(f, slab, other, far_a, far_b):
    g = lax.axis_index("gz")
    low, high = slice(0, PLANES // 2), slice(PLANES // 2, PLANES)

    @pl.when(g == 0)
    def _():
        f[low, ROWS:SPAN, :] = slab[...]
        f[high, ROWS:SPAN, :] = other[...]
        f[low, 0:ROWS, :] = far_a[...]
        f[high, 0:ROWS, :] = far_b[...]

    @pl.when(g == 1)
    def _():
        f[high, 0 : 2 * ROWS, :] = slab[...]
        f[low, 0 : 2 * ROWS, :] = other[...]
        f[high, 2 * ROWS : SPAN, :] = far_a[...]
        f[low, 2 * ROWS : SPAN, :] = far_b[...]


def window_pair(f):
    return lambda p: jnp.concatenate([f[p], f[p + 1]], axis=1)


def strips_pair(far, own, near):
    def pair(p):
        sides = [jnp.concatenate([ref[p], ref[p + 1]], axis=1) for ref in (far, own, near)]
        return jnp.concatenate(sides, axis=0)

    return pair


def chunk_planes(c):
    return pl.ds(c * (CHUNK // ROWS), CHUNK // ROWS)


def as_planes(x):
    return x.reshape(CHUNK // ROWS, ROWS, WIDTH)


def first_pred_kernel(slab, other, far_a, far_b, yw, zf, x1, x2, pred, f, t, u):
    gather_first(f, slab, other, far_a, far_b)
    y_stage(window_pair(f), yw[:, 0:SPAN], filtered_rows(t))
    z_stage(t, u, zf[...])

    def emit(c, x):
        pred[pl.ds(c * CHUNK, CHUNK), :] = x

    x_stage(u, x1[...], x2[...], emit)


def first_ratio_kernel(slab, other, far_a, far_b, yd, xd, shifts, pred, data, ratio, f, d):
    gather_first(f, slab, other, far_a, far_b)
    d[SHIFT : SHIFT + PLANES] = jnp.zeros((PLANES, ROWS, WIDTH), BF16)
    up = SHIFT - shifts[0, 0]

    def put(p, o):
        o = o.astype(BF16)
        d[p + up] = o[:, 0:WIDTH]
        d[p + 1 + up] = o[:, WIDTH : 2 * WIDTH]

    y_stage(window_pair(f), yd[:, 0:SPAN], put)

    def body(c):
        moved = d[pl.ds(SHIFT + c * (CHUNK // ROWS), CHUNK // ROWS)]
        got = dot(moved.reshape(CHUNK, WIDTH), xd[...])
        data[chunk_planes(c)] = as_planes(got).astype(BF16)
        quot = got / (pred[pl.ds(c * CHUNK, CHUNK), :] + 0.05)
        ratio[chunk_planes(c)] = as_planes(quot).astype(BF16)

    loop(FLAT // CHUNK, body)


def back_y_kernel(far, own, near, yb, _, o0, o1, o2, o3, t):
    y_stage(strips_pair(far, own, near), yb[:, 0:SPAN], filtered_rows(t))
    v = lax.axis_index("view")
    for i, out in enumerate((o0, o1, o2, o3)):
        q = lax.rem(v + i, VIEWS) * QUARTER
        for r in range(QUARTER):
            out[r * PLANES : (r + 1) * PLANES, :] = t[
                pl.ds(q + r, PLANES, stride=ROWS), :
            ].astype(BF16)


def compose_kernel(p0, p1, p2, p3, own, c):
    v = lax.axis_index("view")
    for j, ref in enumerate((p0, p1, p2, p3)):
        q = pl.multiple_of(lax.rem(v - j + VIEWS, VIEWS) * QUARTER, QUARTER)
        c[:, pl.ds(q, QUARTER), :] = ref[...].astype(F32)
    own[...] = c[...].astype(BF16)


def next_ratio_kernel(far, own, near, yf, zf, x1, x2, data, ratio, t, u):
    y_stage(strips_pair(far, own, near), yf[:, 0:SPAN], filtered_rows(t))
    z_stage(t, u, zf[...])

    def emit(c, x):
        quot = as_planes(x + 0.05)
        ratio[chunk_planes(c)] = (data[chunk_planes(c)].astype(F32) / quot).astype(BF16)

    x_stage(u, x1[...], x2[...], emit)


def view_count(coverage):
    block = strip_index() * ROWS // BLOCK
    count = coverage[0, block, 0]
    for w in range(1, VIEWS):
        count = count + coverage[w, block, 0]
    return count.astype(F32)


def weighted_total(terms, zb, x1b, x2b, hl):
    both = VIEWS * WIDTH
    for i, term in enumerate(terms):
        zmat = zb[i, :, 0:PLANES]
        high, low = slice(i * WIDTH, (i + 1) * WIDTH), slice(both + i * WIDTH, both + (i + 1) * WIDTH)
        for u in range(QUARTER // 2):
            at = 2 * u * PLANES
            rhs = jnp.concatenate(
                [term[at : at + PLANES, :], term[at + PLANES : at + 2 * PLANES, :]], axis=1
            )
            o = dot(zmat, rhs)
            zh, zl = split(o[0:PLANES] + o[PLANES : 2 * PLANES])
            hl[at : at + PLANES, high] = zh[:, 0:WIDTH]
            hl[at : at + PLANES, low] = zl[:, 0:WIDTH]
            at = at + PLANES
            hl[at : at + PLANES, high] = zh[:, WIDTH : 2 * WIDTH]
            hl[at : at + PLANES, low] = zl[:, WIDTH : 2 * WIDTH]
    return dot(hl[...], x1b[...]) + dot(hl[:, 0:both], x2b[...])


def updated(old, acc, count, new):
    for r in range(QUARTER):
        at = pl.ds(r, PLANES, stride=QUARTER)
        new[at, :] = old[at, :] * acc[r * PLANES : (r + 1) * PLANES, :] / count


def first_update_kernel(
    t0, t1, t2, t3, coverage, mine, theirs, zb, x1b, x2b, field, sent, hl, fq
):
    g = lax.axis_index("gz")
    half = QFLAT // 2

    @pl.when(g == 0)
    def _():
        fq[0:half, :] = mine[...]
        fq[half:QFLAT, :] = theirs[...]

    @pl.when(g == 1)
    def _():
        fq[half:QFLAT, :] = mine[...]
        fq[0:half, :] = theirs[...]

    acc = weighted_total((t0, t1, t2, t3), zb, x1b, x2b, hl)
    updated(fq, acc, view_count(coverage), field)
    sent[...] = field[...].reshape(PLANES, QUARTER, WIDTH).astype(BF16)


def as_rows(x):
    return x[...].astype(F32).reshape(QFLAT, WIDTH)


def last_update_kernel(t0, t1, t2, t3, coverage, old, sent, zb, x1b, x2b, coded, hl, new):
    acc = weighted_total((t0, t1, t2, t3), zb, x1b, x2b, hl)
    updated(old, acc, view_count(coverage), new)
    known = as_rows(sent)

    def total(x):
        return jnp.sum(jnp.sum(x, axis=0, keepdims=True), axis=1, keepdims=True)

    scale = total(new[...] * known) / jnp.maximum(total(known * known), 1e-30)
    scale = scale.astype(BF16).astype(F32)
    coded[0:QFLAT, :] = new[...] - scale * known
    coded[QFLAT : QFLAT + TAIL, :] = jnp.broadcast_to(scale, (TAIL, WIDTH))


def decoded(coded, known, at, lines):
    scale = coded[QFLAT : QFLAT + 1, :]
    value = known[at].astype(F32)
    return coded[lines, :].reshape(value.shape) + scale.reshape(1, 1, WIDTH) * value


def halves_kernel(p0, p1, p2, p3, s0, s1, s2, s3, give):
    g = lax.axis_index("gz")
    half = PLANES // 2
    at = pl.ds((1 - g) * half, half)
    lines = pl.ds(pl.multiple_of((1 - g) * half * QUARTER, half * QUARTER), half * QUARTER)
    for j, (ref, sent) in enumerate(((p0, s0), (p1, s1), (p2, s2), (p3, s3))):
        give[j] = decoded(ref, sent, at, lines)


def final_kernel(p0, p1, p2, p3, s0, s1, s2, s3, got, out):
    v, g = lax.axis_index("view"), lax.axis_index("gz")
    half = PLANES // 2
    at = pl.ds(g * half, half)
    lines = pl.ds(pl.multiple_of(g * half * QUARTER, half * QUARTER), half * QUARTER)
    for j, (ref, sent) in enumerate(((p0, s0), (p1, s1), (p2, s2), (p3, s3))):
        q = lax.rem(v - j + VIEWS, VIEWS) * QUARTER
        here = pl.multiple_of(g * ROWS + q, QUARTER)
        there = pl.multiple_of((1 - g) * ROWS + q, QUARTER)
        out[:, pl.ds(here, QUARTER), :] = decoded(ref, sent, at, lines)
        out[:, pl.ds(there, QUARTER), :] = got[j]


def steps(count, shift):
    return [(i, (i + shift) % count) for i in range(count)]


def on_device(estimate, views, shifts, kernels, coverage):
    strips = lax.axis_size("xy")
    count = 2 * strips
    half = PLANES // 2
    quart = (QFLAT, WIDTH)
    strip = arr((PLANES, ROWS, WIDTH), BF16)
    both = [kernels[0], kernels[0][:, ::-1]]
    taps = jnp.pad(jnp.concatenate(both, axis=0), ((0, 2), (0, WIDTH - kernels.shape[2])))

    piece = arr((half, ROWS, WIDTH), BF16)
    eighth = arr((half, QUARTER, WIDTH), F32)
    eb, em, eo, mine, theirs = call(
        prep_estimate_kernel,
        [arr((half, 2 * ROWS, WIDTH), BF16), piece, piece, eighth, eighth],
    )(estimate)
    vm, vo = call(prep_views_kernel, [piece, piece])(views)

    outward, inward = [], []
    for s in range(strips):
        outward += [(2 * s, 2 * ((s + 1) % strips)), (2 * s + 1, 2 * ((s - 1) % strips) + 1)]
        inward += [(2 * s, 2 * ((s - 1) % strips) + 1), (2 * s + 1, 2 * ((s + 1) % strips))]
    swap = steps(2, 1)
    e_far = [lax.ppermute(eo, STRIPS, outward), lax.ppermute(em, STRIPS, inward)]
    e_all = [eb, lax.ppermute(eb, "gz", swap)] + e_far
    v_far = [lax.ppermute(vo, STRIPS, outward), lax.ppermute(vm, STRIPS, inward)]
    v_all = [views[0], lax.ppermute(views[0], "gz", swap)] + v_far

    yw, yf, yb, zf, x1f, x2f, yd, xd = call(
        own_mats_kernel,
        [
            arr((2 * ROWS, WIDTH), BF16),
            arr((2 * ROWS, WIDTH), BF16),
            arr((2 * ROWS, WIDTH), BF16),
            arr((2 * PLANES, WIDTH), BF16),
            arr((2 * WIDTH, WIDTH), BF16),
            arr((WIDTH, WIDTH), BF16),
            arr((ROWS, WIDTH), BF16),
            arr((WIDTH, WIDTH), BF16),
        ],
        smem=(1,),
    )(taps, shifts)

    window = pltpu.VMEM((PLANES, SPAN, WIDTH), BF16)
    shifted = pltpu.VMEM((PLANES + 2 * SHIFT, ROWS, WIDTH), BF16)
    flat = pltpu.VMEM((FLAT, WIDTH), F32)
    cube = pltpu.VMEM((PLANES, ROWS, WIDTH), F32)
    pairs = pltpu.VMEM((QFLAT, 2 * VIEWS * WIDTH), BF16)
    total = pltpu.VMEM(quart, F32)

    pred = call(first_pred_kernel, arr((FLAT, WIDTH), F32), [window, flat, flat])(
        *e_all, yw, zf, x1f, x2f
    )
    data, ratio = call(first_ratio_kernel, [strip, strip], [window, shifted], smem=(6,))(
        *v_all, yd, xd, shifts, pred
    )

    across = [(i, (i + 1 if i % 2 else i - 1) % count) for i in range(count)]

    def neighbours(x):
        return lax.ppermute(x, STRIPS, across), lax.ppermute(x, "gz", swap)

    def from_views(x):
        return [x] + [lax.ppermute(x, "view", steps(VIEWS, i)) for i in range(1, VIEWS)]

    late, theirs, _ = lax.optimization_barrier((taps, theirs, ratio))
    theirs = lax.ppermute(theirs, "gz", swap)
    zb, x1b, x2b = call(
        all_mats_kernel,
        [
            arr((VIEWS, 2 * PLANES, WIDTH), BF16),
            arr((2 * VIEWS * WIDTH, WIDTH), BF16),
            arr((VIEWS * WIDTH, WIDTH), BF16),
        ],
        smem=(4,),
    )(*from_views(late), coverage)

    field = None
    for step in range(ITERS):
        far, near = neighbours(ratio)
        parts = call(back_y_kernel, [arr(quart, BF16)] * VIEWS, [flat])(far, ratio, near, yb, zb)
        terms = [parts[0]] + [
            lax.ppermute(parts[i], "view", steps(VIEWS, i)) for i in range(1, VIEWS)
        ]
        if step == 0:
            field, sent = call(
                first_update_kernel,
                [arr(quart, F32), arr((PLANES, QUARTER, WIDTH), BF16)],
                [pairs, total],
                smem=(4,),
            )(
                *terms,
                coverage,
                mine.reshape(QFLAT // 2, WIDTH),
                theirs.reshape(QFLAT // 2, WIDTH),
                zb,
                x1b,
                x2b,
            )
            sent = from_views(sent)
            own = call(compose_kernel, strip, [cube])(*sent)
            far, near = neighbours(own)
            ratio = call(next_ratio_kernel, strip, [flat, flat])(
                far, own, near, yf, zf, x1f, x2f, data
            )
        else:
            coded = call(
                last_update_kernel,
                arr((QFLAT + TAIL, WIDTH), F32),
                [pairs, total],
                smem=(4,),
            )(*terms, coverage, field, sent[0], zb, x1b, x2b)
    coded = lax.optimization_barrier(coded.astype(F16))
    pieces = [lax.optimization_barrier(x).astype(F32) for x in from_views(coded)]
    give = call(halves_kernel, arr((VIEWS, half, QUARTER, WIDTH), F32))(*pieces, *sent)
    got = lax.ppermute(give, "gz", swap)
    return call(final_kernel, arr((half, 2 * ROWS, WIDTH), F32))(*pieces, *sent, got)


def solution(mesh):
    placed = (
        P("gz", "xy", None),
        P("view", "gz", "xy", None),
        P("view", None),
        P("view", None, None),
        P(),
    )
    return jax.shard_map(
        on_device, mesh=mesh, in_specs=placed, out_specs=P("gz", "xy", None), check_vma=False
    )
```

```python
import jax
import jax.numpy as jnp
from jax import lax
from jax.experimental import pallas as pl
from jax.experimental.pallas import tpu as pltpu
from jax.sharding import PartitionSpec as P


F32 = jnp.float32
BF16 = jnp.bfloat16
F16 = jnp.float16
ITERS = 2
VIEWS = 4
PLANES = 64
ROWS = 32
WIDTH = 128
SPAN = 3 * ROWS
QUARTER = ROWS // VIEWS
FLAT = ROWS * PLANES
QFLAT = QUARTER * PLANES
HALF = 31
SHIFT = 32
CHUNK = 512
TAIL = 8
BLOCK = 128
STRIPS = ("xy", "gz")


def dot(a, b):
    return jnp.dot(a, b, preferred_element_type=F32)


def split(x):
    high = x.astype(BF16)
    return high, (x - high.astype(F32)).astype(BF16)


def call(kernel, outs, scratch=(), flops=10**8, smem=()):
    def space(i):
        return pltpu.SMEM if i in smem else pltpu.VMEM

    def run(*args):
        specs = [pl.BlockSpec(memory_space=space(i)) for i in range(len(args))]
        one = not isinstance(outs, (list, tuple))
        shapes = [outs] if one else list(outs)
        made = pl.pallas_call(
            kernel,
            out_shape=shapes,
            in_specs=specs,
            out_specs=[pl.BlockSpec(memory_space=pltpu.VMEM)] * len(shapes),
            scratch_shapes=list(scratch),
            compiler_params=pltpu.CompilerParams(vmem_limit_bytes=16 << 20),
            cost_estimate=pl.CostEstimate(flops=flops, bytes_accessed=4 << 20, transcendentals=0),
        )(*args)
        return made[0] if one else made

    return run


def loop(count, body):
    for c in range(count):
        body(c)


def arr(shape, dtype):
    return jax.ShapeDtypeStruct(shape, dtype)


def strip_index():
    return lax.axis_index("xy") * 2 + lax.axis_index("gz")


def prep_estimate_kernel(est, eb, em, eo, mine, theirs):
    v, g = lax.axis_index("view"), lax.axis_index("gz")
    eb[...] = est[...].astype(BF16)

    @pl.when(g == 0)
    def _():
        em[...] = est[:, 0:ROWS, :].astype(BF16)
        eo[...] = est[:, ROWS : 2 * ROWS, :].astype(BF16)

    @pl.when(g == 1)
    def _():
        eo[...] = est[:, 0:ROWS, :].astype(BF16)
        em[...] = est[:, ROWS : 2 * ROWS, :].astype(BF16)

    here = pl.multiple_of(g * ROWS + v * QUARTER, QUARTER)
    there = pl.multiple_of((1 - g) * ROWS + v * QUARTER, QUARTER)
    mine[...] = est[:, pl.ds(here, QUARTER), :]
    theirs[...] = est[:, pl.ds(there, QUARTER), :]


def prep_views_kernel(views, vm, vo):
    g = lax.axis_index("gz")

    @pl.when(g == 0)
    def _():
        vm[...] = views[0, :, 0:ROWS, :]
        vo[...] = views[0, :, ROWS : 2 * ROWS, :]

    @pl.when(g == 1)
    def _():
        vo[...] = views[0, :, 0:ROWS, :]
        vm[...] = views[0, :, ROWS : 2 * ROWS, :]


def toeplitz(row, rows, shift):
    return pltpu.roll(jnp.broadcast_to(row, (rows, WIDTH)), shift, 1, stride=1, stride_axis=0)


def normed(taps):
    return taps / jnp.sum(taps, axis=1, keepdims=True)


def x_matrix(row):
    i = lax.broadcasted_iota(jnp.int32, (WIDTH, WIDTH), 0)
    j = lax.broadcasted_iota(jnp.int32, (WIDTH, WIDTH), 1)
    full = toeplitz(row, WIDTH, WIDTH - HALF)
    return jnp.where(jnp.abs(i - j) <= HALF, full, 0.0)


def row_valid(rows):
    r = strip_index()
    j = lax.broadcasted_iota(jnp.int32, (rows, WIDTH), 1)
    low = jnp.where(r == 0, ROWS, 0)
    high = jnp.where(r == 2 * lax.axis_size("xy") - 1, 2 * ROWS, SPAN)
    return (j >= low) & (j < high)


def own_mats_kernel(taps, shifts, yw, yf, yb, zf, x1f, x2f, yd, xd):
    k = normed(taps[...])
    valid = row_valid(ROWS)
    column = lax.broadcasted_iota(jnp.int32, (ROWS, WIDTH), 1)
    kept = (lax.axis_index("gz") == 0) | ((column >= ROWS) & (column < 2 * ROWS))

    def sides(y):
        return jnp.where(kept, y, pltpu.roll(y, 2 * ROWS, 1))

    forward = jnp.where(valid, toeplitz(k[1:2], ROWS, 1), 0.0)
    backward = jnp.where(valid, toeplitz(k[4:5], ROWS, 1), 0.0)
    for ref, y in ((yw, forward), (yf, sides(forward)), (yb, sides(backward))):
        h, l = split(y)
        ref[0:ROWS, :] = h
        ref[ROWS : 2 * ROWS, :] = l
    lane = lax.broadcasted_iota(jnp.int32, (PLANES, WIDTH), 1)
    z = jnp.where(lane < PLANES, toeplitz(k[0:1], PLANES, WIDTH - HALF), 0.0)
    zh = z.astype(BF16).astype(F32)
    zf[0:PLANES, :] = (zh + pltpu.roll(zh, PLANES, 1)).astype(BF16)
    zf[PLANES : 2 * PLANES, :] = (z - zh).astype(BF16)
    h, l = split(x_matrix(k[5:6]))
    x1f[0:WIDTH, :] = h
    x1f[WIDTH : 2 * WIDTH, :] = h
    x2f[...] = l

    def hot(rows, offset):
        i = lax.broadcasted_iota(jnp.int32, (rows, WIDTH), 0)
        j = lax.broadcasted_iota(jnp.int32, (rows, WIDTH), 1)
        return jnp.where(j - i == offset, 1.0, 0.0)

    yd[...] = jnp.where(valid, hot(ROWS, shifts[0, 1] + ROWS), 0.0).astype(BF16)
    xd[...] = hot(WIDTH, -shifts[0, 2]).astype(BF16)


def all_mats_kernel(t0, t1, t2, t3, coverage, zb, x1b, x2b):
    v = lax.axis_index("view")
    block = strip_index() * ROWS // BLOCK
    for i, taps in enumerate((t0, t1, t2, t3)):
        k = normed(taps[...])
        zh, zl = split(toeplitz(k[3:4], PLANES, WIDTH - HALF))
        zb[i, 0:PLANES, :] = zh
        zb[i, PLANES : 2 * PLANES, :] = zl
        weight = coverage[lax.rem(v - i + VIEWS, VIEWS), block, 0].astype(F32)
        h, l = split(weight * x_matrix(k[2:3]))
        at = slice(i * WIDTH, (i + 1) * WIDTH)
        x1b[at, :] = h
        x1b[VIEWS * WIDTH + i * WIDTH : VIEWS * WIDTH + (i + 1) * WIDTH, :] = h
        x2b[at, :] = l


def y_stage(pair, matrix, put):
    loop(PLANES // 2, lambda c: put(2 * c, dot(matrix, pair(2 * c))))


def filtered_rows(t):
    def put(p, o):
        o = o[0:ROWS] + o[ROWS : 2 * ROWS]
        t[pl.ds(p * ROWS, ROWS), :] = o[:, 0:WIDTH]
        t[pl.ds(p * ROWS + ROWS, ROWS), :] = o[:, WIDTH : 2 * WIDTH]

    return put


def z_stage(t, u, zf):
    def body(c):
        first, second = (pl.ds(2 * c + k, PLANES, stride=ROWS) for k in (0, 1))
        h0, l0 = split(t[first, :])
        h1, l1 = split(t[second, :])
        rhs = jnp.concatenate(
            [jnp.concatenate([h0, h1], axis=1), jnp.concatenate([l0, l1], axis=1)], axis=0
        )
        o = dot(zf, rhs)
        o = o[0:PLANES] + o[PLANES : 2 * PLANES]
        u[first, :] = o[:, 0:WIDTH]
        u[second, :] = o[:, WIDTH : 2 * WIDTH]

    loop(ROWS // 2, body)


def x_stage(t, x1, x2, emit):
    def body(c):
        h, l = split(t[pl.ds(c * CHUNK, CHUNK), :])
        emit(c, dot(jnp.concatenate([h, l], axis=1), x1) + dot(h, x2))

    loop(FLAT // CHUNK, body)


def gather_first(f, slab, other, far_a, far_b):
    g = lax.axis_index("gz")
    low, high = slice(0, PLANES // 2), slice(PLANES // 2, PLANES)

    @pl.when(g == 0)
    def _():
        f[low, ROWS:SPAN, :] = slab[...]
        f[high, ROWS:SPAN, :] = other[...]
        f[low, 0:ROWS, :] = far_a[...]
        f[high, 0:ROWS, :] = far_b[...]

    @pl.when(g == 1)
    def _():
        f[high, 0 : 2 * ROWS, :] = slab[...]
        f[low, 0 : 2 * ROWS, :] = other[...]
        f[high, 2 * ROWS : SPAN, :] = far_a[...]
        f[low, 2 * ROWS : SPAN, :] = far_b[...]


def window_pair(f):
    return lambda p: jnp.concatenate([f[p], f[p + 1]], axis=1)


def strips_pair(far, own, near):
    def pair(p):
        sides = [jnp.concatenate([ref[p], ref[p + 1]], axis=1) for ref in (far, own, near)]
        return jnp.concatenate(sides, axis=0)

    return pair


def chunk_planes(c):
    return pl.ds(c * (CHUNK // ROWS), CHUNK // ROWS)


def as_planes(x):
    return x.reshape(CHUNK // ROWS, ROWS, WIDTH)


def first_pred_kernel(slab, other, far_a, far_b, yw, zf, x1, x2, pred, f, t, u):
    gather_first(f, slab, other, far_a, far_b)
    y_stage(window_pair(f), yw[:, 0:SPAN], filtered_rows(t))
    z_stage(t, u, zf[...])

    def emit(c, x):
        pred[pl.ds(c * CHUNK, CHUNK), :] = x

    x_stage(u, x1[...], x2[...], emit)


def first_ratio_kernel(slab, other, far_a, far_b, yd, xd, shifts, pred, data, ratio, f, d):
    gather_first(f, slab, other, far_a, far_b)
    d[SHIFT : SHIFT + PLANES] = jnp.zeros((PLANES, ROWS, WIDTH), BF16)
    up = SHIFT - shifts[0, 0]

    def put(p, o):
        o = o.astype(BF16)
        d[p + up] = o[:, 0:WIDTH]
        d[p + 1 + up] = o[:, WIDTH : 2 * WIDTH]

    y_stage(window_pair(f), yd[:, 0:SPAN], put)

    def body(c):
        moved = d[pl.ds(SHIFT + c * (CHUNK // ROWS), CHUNK // ROWS)]
        got = dot(moved.reshape(CHUNK, WIDTH), xd[...])
        data[chunk_planes(c)] = as_planes(got).astype(BF16)
        quot = got / (pred[pl.ds(c * CHUNK, CHUNK), :] + 0.05)
        ratio[chunk_planes(c)] = as_planes(quot).astype(BF16)

    loop(FLAT // CHUNK, body)


def back_y_kernel(far, own, near, yb, _, o0, o1, o2, o3, t):
    y_stage(strips_pair(far, own, near), yb[:, 0:SPAN], filtered_rows(t))
    v = lax.axis_index("view")
    for i, out in enumerate((o0, o1, o2, o3)):
        q = lax.rem(v + i, VIEWS) * QUARTER
        for r in range(QUARTER):
            out[r * PLANES : (r + 1) * PLANES, :] = t[
                pl.ds(q + r, PLANES, stride=ROWS), :
            ].astype(BF16)


def compose_kernel(p0, p1, p2, p3, own, c):
    v = lax.axis_index("view")
    for j, ref in enumerate((p0, p1, p2, p3)):
        q = pl.multiple_of(lax.rem(v - j + VIEWS, VIEWS) * QUARTER, QUARTER)
        c[:, pl.ds(q, QUARTER), :] = ref[...].astype(F32)
    own[...] = c[...].astype(BF16)


def next_ratio_kernel(far, own, near, yf, zf, x1, x2, data, ratio, t, u):
    y_stage(strips_pair(far, own, near), yf[:, 0:SPAN], filtered_rows(t))
    z_stage(t, u, zf[...])

    def emit(c, x):
        quot = as_planes(x + 0.05)
        ratio[chunk_planes(c)] = (data[chunk_planes(c)].astype(F32) / quot).astype(BF16)

    x_stage(u, x1[...], x2[...], emit)


def view_count(coverage):
    block = strip_index() * ROWS // BLOCK
    count = coverage[0, block, 0]
    for w in range(1, VIEWS):
        count = count + coverage[w, block, 0]
    return count.astype(F32)


def weighted_total(terms, zb, x1b, x2b, hl):
    both = VIEWS * WIDTH
    for i, term in enumerate(terms):
        zmat = zb[i, :, 0:PLANES]
        high, low = slice(i * WIDTH, (i + 1) * WIDTH), slice(both + i * WIDTH, both + (i + 1) * WIDTH)
        for u in range(QUARTER // 2):
            at = 2 * u * PLANES
            rhs = jnp.concatenate(
                [term[at : at + PLANES, :], term[at + PLANES : at + 2 * PLANES, :]], axis=1
            )
            o = dot(zmat, rhs)
            zh, zl = split(o[0:PLANES] + o[PLANES : 2 * PLANES])
            hl[at : at + PLANES, high] = zh[:, 0:WIDTH]
            hl[at : at + PLANES, low] = zl[:, 0:WIDTH]
            at = at + PLANES
            hl[at : at + PLANES, high] = zh[:, WIDTH : 2 * WIDTH]
            hl[at : at + PLANES, low] = zl[:, WIDTH : 2 * WIDTH]
    return dot(hl[...], x1b[...]) + dot(hl[:, 0:both], x2b[...])


def updated(old, acc, count, new):
    for r in range(QUARTER):
        at = pl.ds(r, PLANES, stride=QUARTER)
        new[at, :] = old[at, :] * acc[r * PLANES : (r + 1) * PLANES, :] / count


def first_update_kernel(
    t0, t1, t2, t3, coverage, mine, theirs, zb, x1b, x2b, field, sent, hl, fq
):
    g = lax.axis_index("gz")
    half = QFLAT // 2

    @pl.when(g == 0)
    def _():
        fq[0:half, :] = mine[...]
        fq[half:QFLAT, :] = theirs[...]

    @pl.when(g == 1)
    def _():
        fq[half:QFLAT, :] = mine[...]
        fq[0:half, :] = theirs[...]

    acc = weighted_total((t0, t1, t2, t3), zb, x1b, x2b, hl)
    updated(fq, acc, view_count(coverage), field)
    sent[...] = field[...].reshape(PLANES, QUARTER, WIDTH).astype(BF16)


def as_rows(x):
    return x[...].astype(F32).reshape(QFLAT, WIDTH)


def last_update_kernel(t0, t1, t2, t3, coverage, old, sent, zb, x1b, x2b, coded, hl, new):
    acc = weighted_total((t0, t1, t2, t3), zb, x1b, x2b, hl)
    updated(old, acc, view_count(coverage), new)
    known = as_rows(sent)

    def total(x):
        return jnp.sum(jnp.sum(x, axis=0, keepdims=True), axis=1, keepdims=True)

    scale = total(new[...] * known) / jnp.maximum(total(known * known), 1e-30)
    scale = scale.astype(BF16).astype(F32)
    coded[0:QFLAT, :] = new[...] - scale * known
    coded[QFLAT : QFLAT + TAIL, :] = jnp.broadcast_to(scale, (TAIL, WIDTH))


def decoded(coded, known, at, lines):
    scale = coded[QFLAT : QFLAT + 1, :]
    value = known[at].astype(F32)
    return coded[lines, :].reshape(value.shape) + scale.reshape(1, 1, WIDTH) * value


def halves_kernel(p0, p1, p2, p3, s0, s1, s2, s3, give):
    g = lax.axis_index("gz")
    half = PLANES // 2
    at = pl.ds((1 - g) * half, half)
    lines = pl.ds(pl.multiple_of((1 - g) * half * QUARTER, half * QUARTER), half * QUARTER)
    for j, (ref, sent) in enumerate(((p0, s0), (p1, s1), (p2, s2), (p3, s3))):
        give[j] = decoded(ref, sent, at, lines)


def final_kernel(p0, p1, p2, p3, s0, s1, s2, s3, got, out):
    v, g = lax.axis_index("view"), lax.axis_index("gz")
    half = PLANES // 2
    at = pl.ds(g * half, half)
    lines = pl.ds(pl.multiple_of(g * half * QUARTER, half * QUARTER), half * QUARTER)
    for j, (ref, sent) in enumerate(((p0, s0), (p1, s1), (p2, s2), (p3, s3))):
        q = lax.rem(v - j + VIEWS, VIEWS) * QUARTER
        here = pl.multiple_of(g * ROWS + q, QUARTER)
        there = pl.multiple_of((1 - g) * ROWS + q, QUARTER)
        out[:, pl.ds(here, QUARTER), :] = decoded(ref, sent, at, lines)
        out[:, pl.ds(there, QUARTER), :] = got[j]


def steps(count, shift):
    return [(i, (i + shift) % count) for i in range(count)]


def on_device(estimate, views, shifts, kernels, coverage):
    strips = lax.axis_size("xy")
    count = 2 * strips
    half = PLANES // 2
    quart = (QFLAT, WIDTH)
    strip = arr((PLANES, ROWS, WIDTH), BF16)
    both = [kernels[0], kernels[0][:, ::-1]]
    taps = jnp.pad(jnp.concatenate(both, axis=0), ((0, 2), (0, WIDTH - kernels.shape[2])))

    piece = arr((half, ROWS, WIDTH), BF16)
    eighth = arr((half, QUARTER, WIDTH), F32)
    eb, em, eo, mine, theirs = call(
        prep_estimate_kernel,
        [arr((half, 2 * ROWS, WIDTH), BF16), piece, piece, eighth, eighth],
    )(estimate)
    vm, vo = call(prep_views_kernel, [piece, piece])(views)

    outward, inward = [], []
    for s in range(strips):
        outward += [(2 * s, 2 * ((s + 1) % strips)), (2 * s + 1, 2 * ((s - 1) % strips) + 1)]
        inward += [(2 * s, 2 * ((s - 1) % strips) + 1), (2 * s + 1, 2 * ((s + 1) % strips))]
    swap = steps(2, 1)
    e_far = [lax.ppermute(eo, STRIPS, outward), lax.ppermute(em, STRIPS, inward)]
    e_all = [eb, lax.ppermute(eb, "gz", swap)] + e_far
    v_far = [lax.ppermute(vo, STRIPS, outward), lax.ppermute(vm, STRIPS, inward)]
    v_all = [views[0], lax.ppermute(views[0], "gz", swap)] + v_far

    yw, yf, yb, zf, x1f, x2f, yd, xd = call(
        own_mats_kernel,
        [
            arr((2 * ROWS, WIDTH), BF16),
            arr((2 * ROWS, WIDTH), BF16),
            arr((2 * ROWS, WIDTH), BF16),
            arr((2 * PLANES, WIDTH), BF16),
            arr((2 * WIDTH, WIDTH), BF16),
            arr((WIDTH, WIDTH), BF16),
            arr((ROWS, WIDTH), BF16),
            arr((WIDTH, WIDTH), BF16),
        ],
        smem=(1,),
    )(taps, shifts)

    window = pltpu.VMEM((PLANES, SPAN, WIDTH), BF16)
    shifted = pltpu.VMEM((PLANES + 2 * SHIFT, ROWS, WIDTH), BF16)
    flat = pltpu.VMEM((FLAT, WIDTH), F32)
    cube = pltpu.VMEM((PLANES, ROWS, WIDTH), F32)
    pairs = pltpu.VMEM((QFLAT, 2 * VIEWS * WIDTH), BF16)
    total = pltpu.VMEM(quart, F32)

    pred = call(first_pred_kernel, arr((FLAT, WIDTH), F32), [window, flat, flat])(
        *e_all, yw, zf, x1f, x2f
    )
    data, ratio = call(first_ratio_kernel, [strip, strip], [window, shifted], smem=(6,))(
        *v_all, yd, xd, shifts, pred
    )

    across = [(i, (i + 1 if i % 2 else i - 1) % count) for i in range(count)]

    def neighbours(x):
        return lax.ppermute(x, STRIPS, across), lax.ppermute(x, "gz", swap)

    def from_views(x):
        return [x] + [lax.ppermute(x, "view", steps(VIEWS, i)) for i in range(1, VIEWS)]

    late, theirs, _ = lax.optimization_barrier((taps, theirs, ratio))
    theirs = lax.ppermute(theirs, "gz", swap)
    zb, x1b, x2b = call(
        all_mats_kernel,
        [
            arr((VIEWS, 2 * PLANES, WIDTH), BF16),
            arr((2 * VIEWS * WIDTH, WIDTH), BF16),
            arr((VIEWS * WIDTH, WIDTH), BF16),
        ],
        smem=(4,),
    )(*from_views(late), coverage)

    field = None
    for step in range(ITERS):
        far, near = neighbours(ratio)
        parts = call(back_y_kernel, [arr(quart, BF16)] * VIEWS, [flat])(far, ratio, near, yb, zb)
        terms = [parts[0]] + [
            lax.ppermute(parts[i], "view", steps(VIEWS, i)) for i in range(1, VIEWS)
        ]
        if step == 0:
            field, sent = call(
                first_update_kernel,
                [arr(quart, F32), arr((PLANES, QUARTER, WIDTH), BF16)],
                [pairs, total],
                smem=(4,),
            )(
                *terms,
                coverage,
                mine.reshape(QFLAT // 2, WIDTH),
                theirs.reshape(QFLAT // 2, WIDTH),
                zb,
                x1b,
                x2b,
            )
            beyond = lax.ppermute(sent, STRIPS, across)
            sent = from_views(sent)
            outer = from_views(beyond)
            own = call(compose_kernel, strip, [cube])(*sent)
            near = lax.ppermute(own, "gz", swap)
            far = call(compose_kernel, strip, [cube])(*outer)
            ratio = call(next_ratio_kernel, strip, [flat, flat])(
                far, own, near, yf, zf, x1f, x2f, data
            )
        else:
            coded = call(
                last_update_kernel,
                arr((QFLAT + TAIL, WIDTH), F32),
                [pairs, total],
                smem=(4,),
            )(*terms, coverage, field, sent[0], zb, x1b, x2b)
    coded = lax.optimization_barrier(coded.astype(F16))
    pieces = [lax.optimization_barrier(x).astype(F32) for x in from_views(coded)]
    give = call(halves_kernel, arr((VIEWS, half, QUARTER, WIDTH), F32))(*pieces, *sent)
    got = lax.ppermute(give, "gz", swap)
    return call(final_kernel, arr((half, 2 * ROWS, WIDTH), F32))(*pieces, *sent, got)


def solution(mesh):
    placed = (
        P("gz", "xy", None),
        P("view", "gz", "xy", None),
        P("view", None),
        P("view", None, None),
        P(),
    )
    return jax.shard_map(
        on_device, mesh=mesh, in_specs=placed, out_specs=P("gz", "xy", None), check_vma=False
    )
```

```python
import jax
import jax.numpy as jnp
from jax import lax
from jax.experimental import pallas as pl
from jax.experimental.pallas import tpu as pltpu
from jax.sharding import PartitionSpec as P


F32 = jnp.float32
BF16 = jnp.bfloat16
F16 = jnp.float16
ITERS = 2
VIEWS = 4
PLANES = 64
ROWS = 32
WIDTH = 128
SPAN = 3 * ROWS
QUARTER = ROWS // VIEWS
FLAT = ROWS * PLANES
QFLAT = QUARTER * PLANES
HALF = 31
SHIFT = 32
CHUNK = 512
TAIL = 8
BLOCK = 128
STRIPS = ("xy", "gz")


def dot(a, b):
    return jnp.dot(a, b, preferred_element_type=F32)


def split(x):
    high = x.astype(BF16)
    return high, (x - high.astype(F32)).astype(BF16)


def call(kernel, outs, scratch=(), flops=10**8, smem=()):
    def space(i):
        return pltpu.SMEM if i in smem else pltpu.VMEM

    def run(*args):
        specs = [pl.BlockSpec(memory_space=space(i)) for i in range(len(args))]
        one = not isinstance(outs, (list, tuple))
        shapes = [outs] if one else list(outs)
        made = pl.pallas_call(
            kernel,
            out_shape=shapes,
            in_specs=specs,
            out_specs=[pl.BlockSpec(memory_space=pltpu.VMEM)] * len(shapes),
            scratch_shapes=list(scratch),
            compiler_params=pltpu.CompilerParams(vmem_limit_bytes=16 << 20),
            cost_estimate=pl.CostEstimate(flops=flops, bytes_accessed=4 << 20, transcendentals=0),
        )(*args)
        return made[0] if one else made

    return run


def loop(count, body):
    for c in range(count):
        body(c)


def arr(shape, dtype):
    return jax.ShapeDtypeStruct(shape, dtype)


def strip_index():
    return lax.axis_index("xy") * 2 + lax.axis_index("gz")


def prep_estimate_kernel(est, eb, em, eo, mine, theirs):
    v, g = lax.axis_index("view"), lax.axis_index("gz")
    eb[...] = est[...].astype(BF16)

    @pl.when(g == 0)
    def _():
        em[...] = est[:, 0:ROWS, :].astype(BF16)
        eo[...] = est[:, ROWS : 2 * ROWS, :].astype(BF16)

    @pl.when(g == 1)
    def _():
        eo[...] = est[:, 0:ROWS, :].astype(BF16)
        em[...] = est[:, ROWS : 2 * ROWS, :].astype(BF16)

    here = pl.multiple_of(g * ROWS + v * QUARTER, QUARTER)
    there = pl.multiple_of((1 - g) * ROWS + v * QUARTER, QUARTER)
    mine[...] = est[:, pl.ds(here, QUARTER), :]
    theirs[...] = est[:, pl.ds(there, QUARTER), :]


def prep_views_kernel(views, vm, vo):
    g = lax.axis_index("gz")

    @pl.when(g == 0)
    def _():
        vm[...] = views[0, :, 0:ROWS, :]
        vo[...] = views[0, :, ROWS : 2 * ROWS, :]

    @pl.when(g == 1)
    def _():
        vo[...] = views[0, :, 0:ROWS, :]
        vm[...] = views[0, :, ROWS : 2 * ROWS, :]


def toeplitz(row, rows, shift):
    return pltpu.roll(jnp.broadcast_to(row, (rows, WIDTH)), shift, 1, stride=1, stride_axis=0)


def normed(taps):
    return taps / jnp.sum(taps, axis=1, keepdims=True)


def x_matrix(row):
    i = lax.broadcasted_iota(jnp.int32, (WIDTH, WIDTH), 0)
    j = lax.broadcasted_iota(jnp.int32, (WIDTH, WIDTH), 1)
    full = toeplitz(row, WIDTH, WIDTH - HALF)
    return jnp.where(jnp.abs(i - j) <= HALF, full, 0.0)


def row_valid(rows):
    r = strip_index()
    j = lax.broadcasted_iota(jnp.int32, (rows, WIDTH), 1)
    low = jnp.where(r == 0, ROWS, 0)
    high = jnp.where(r == 2 * lax.axis_size("xy") - 1, 2 * ROWS, SPAN)
    return (j >= low) & (j < high)


def own_mats_kernel(taps, shifts, yw, yf, yb, zf, x1f, x2f, yd, xd):
    k = normed(taps[...])
    valid = row_valid(ROWS)
    column = lax.broadcasted_iota(jnp.int32, (ROWS, WIDTH), 1)
    kept = (lax.axis_index("gz") == 0) | ((column >= ROWS) & (column < 2 * ROWS))

    def sides(y):
        return jnp.where(kept, y, pltpu.roll(y, 2 * ROWS, 1))

    forward = jnp.where(valid, toeplitz(k[1:2], ROWS, 1), 0.0)
    backward = jnp.where(valid, toeplitz(k[4:5], ROWS, 1), 0.0)
    for ref, y in ((yw, forward), (yf, sides(forward)), (yb, sides(backward))):
        h, l = split(y)
        ref[0:ROWS, :] = h
        ref[ROWS : 2 * ROWS, :] = l
    lane = lax.broadcasted_iota(jnp.int32, (PLANES, WIDTH), 1)
    z = jnp.where(lane < PLANES, toeplitz(k[0:1], PLANES, WIDTH - HALF), 0.0)
    zh = z.astype(BF16).astype(F32)
    zf[0:PLANES, :] = (zh + pltpu.roll(zh, PLANES, 1)).astype(BF16)
    zf[PLANES : 2 * PLANES, :] = (z - zh).astype(BF16)
    h, l = split(x_matrix(k[5:6]))
    x1f[0:WIDTH, :] = h
    x1f[WIDTH : 2 * WIDTH, :] = h
    x2f[...] = l

    def hot(rows, offset):
        i = lax.broadcasted_iota(jnp.int32, (rows, WIDTH), 0)
        j = lax.broadcasted_iota(jnp.int32, (rows, WIDTH), 1)
        return jnp.where(j - i == offset, 1.0, 0.0)

    yd[...] = jnp.where(valid, hot(ROWS, shifts[0, 1] + ROWS), 0.0).astype(BF16)
    xd[...] = hot(WIDTH, -shifts[0, 2]).astype(BF16)


def all_mats_kernel(t0, t1, t2, t3, coverage, zb, x1b, x2b):
    v = lax.axis_index("view")
    block = strip_index() * ROWS // BLOCK
    for i, taps in enumerate((t0, t1, t2, t3)):
        k = normed(taps[...])
        zh, zl = split(toeplitz(k[3:4], PLANES, WIDTH - HALF))
        zb[i, 0:PLANES, :] = zh
        zb[i, PLANES : 2 * PLANES, :] = zl
        weight = coverage[lax.rem(v - i + VIEWS, VIEWS), block, 0].astype(F32)
        h, l = split(weight * x_matrix(k[2:3]))
        at = slice(i * WIDTH, (i + 1) * WIDTH)
        x1b[at, :] = h
        x1b[VIEWS * WIDTH + i * WIDTH : VIEWS * WIDTH + (i + 1) * WIDTH, :] = h
        x2b[at, :] = l


def y_stage(pair, matrix, put):
    loop(PLANES // 2, lambda c: put(2 * c, dot(matrix, pair(2 * c))))


def filtered_rows(t):
    def put(p, o):
        o = o[0:ROWS] + o[ROWS : 2 * ROWS]
        t[pl.ds(p * ROWS, ROWS), :] = o[:, 0:WIDTH]
        t[pl.ds(p * ROWS + ROWS, ROWS), :] = o[:, WIDTH : 2 * WIDTH]

    return put


def z_stage(t, u, zf):
    def body(c):
        first, second = (pl.ds(2 * c + k, PLANES, stride=ROWS) for k in (0, 1))
        h0, l0 = split(t[first, :])
        h1, l1 = split(t[second, :])
        rhs = jnp.concatenate(
            [jnp.concatenate([h0, h1], axis=1), jnp.concatenate([l0, l1], axis=1)], axis=0
        )
        o = dot(zf, rhs)
        o = o[0:PLANES] + o[PLANES : 2 * PLANES]
        u[first, :] = o[:, 0:WIDTH]
        u[second, :] = o[:, WIDTH : 2 * WIDTH]

    loop(ROWS // 2, body)


def x_stage(t, x1, x2, emit):
    def body(c):
        h, l = split(t[pl.ds(c * CHUNK, CHUNK), :])
        emit(c, dot(jnp.concatenate([h, l], axis=1), x1) + dot(h, x2))

    loop(FLAT // CHUNK, body)


def gather_first(f, slab, other, far_a, far_b):
    g = lax.axis_index("gz")
    low, high = slice(0, PLANES // 2), slice(PLANES // 2, PLANES)

    @pl.when(g == 0)
    def _():
        f[low, ROWS:SPAN, :] = slab[...]
        f[high, ROWS:SPAN, :] = other[...]
        f[low, 0:ROWS, :] = far_a[...]
        f[high, 0:ROWS, :] = far_b[...]

    @pl.when(g == 1)
    def _():
        f[high, 0 : 2 * ROWS, :] = slab[...]
        f[low, 0 : 2 * ROWS, :] = other[...]
        f[high, 2 * ROWS : SPAN, :] = far_a[...]
        f[low, 2 * ROWS : SPAN, :] = far_b[...]


def window_pair(f):
    return lambda p: jnp.concatenate([f[p], f[p + 1]], axis=1)


def strips_pair(far, own, near):
    def pair(p):
        sides = [jnp.concatenate([ref[p], ref[p + 1]], axis=1) for ref in (far, own, near)]
        return jnp.concatenate(sides, axis=0)

    return pair


def chunk_planes(c):
    return pl.ds(c * (CHUNK // ROWS), CHUNK // ROWS)


def as_planes(x):
    return x.reshape(CHUNK // ROWS, ROWS, WIDTH)


def first_pred_kernel(slab, other, far_a, far_b, yw, zf, x1, x2, pred, f, t, u):
    gather_first(f, slab, other, far_a, far_b)
    y_stage(window_pair(f), yw[:, 0:SPAN], filtered_rows(t))
    z_stage(t, u, zf[...])

    def emit(c, x):
        pred[pl.ds(c * CHUNK, CHUNK), :] = x

    x_stage(u, x1[...], x2[...], emit)


def first_ratio_kernel(slab, other, far_a, far_b, yd, xd, shifts, pred, data, ratio, f, d):
    gather_first(f, slab, other, far_a, far_b)
    d[SHIFT : SHIFT + PLANES] = jnp.zeros((PLANES, ROWS, WIDTH), BF16)
    up = SHIFT - shifts[0, 0]

    def put(p, o):
        o = o.astype(BF16)
        d[p + up] = o[:, 0:WIDTH]
        d[p + 1 + up] = o[:, WIDTH : 2 * WIDTH]

    y_stage(window_pair(f), yd[:, 0:SPAN], put)

    def body(c):
        moved = d[pl.ds(SHIFT + c * (CHUNK // ROWS), CHUNK // ROWS)]
        got = dot(moved.reshape(CHUNK, WIDTH), xd[...])
        data[chunk_planes(c)] = as_planes(got).astype(BF16)
        quot = got / (pred[pl.ds(c * CHUNK, CHUNK), :] + 0.05)
        ratio[chunk_planes(c)] = as_planes(quot).astype(BF16)

    loop(FLAT // CHUNK, body)


def back_y_kernel(far, own, near, yb, *refs):
    o0, o1, o2, o3, t = refs[-5:]
    y_stage(strips_pair(far, own, near), yb[:, 0:SPAN], filtered_rows(t))
    v = lax.axis_index("view")
    for i, out in enumerate((o0, o1, o2, o3)):
        q = lax.rem(v + i, VIEWS) * QUARTER
        for r in range(QUARTER):
            out[r * PLANES : (r + 1) * PLANES, :] = t[
                pl.ds(q + r, PLANES, stride=ROWS), :
            ].astype(BF16)


def compose_kernel(p0, p1, p2, p3, own, c):
    v = lax.axis_index("view")
    for j, ref in enumerate((p0, p1, p2, p3)):
        q = pl.multiple_of(lax.rem(v - j + VIEWS, VIEWS) * QUARTER, QUARTER)
        c[:, pl.ds(q, QUARTER), :] = ref[...].astype(F32)
    own[...] = c[...].astype(BF16)


def next_ratio_kernel(far, own, near, yf, zf, x1, x2, data, ratio, t, u):
    y_stage(strips_pair(far, own, near), yf[:, 0:SPAN], filtered_rows(t))
    z_stage(t, u, zf[...])

    def emit(c, x):
        quot = as_planes(x + 0.05)
        ratio[chunk_planes(c)] = (data[chunk_planes(c)].astype(F32) / quot).astype(BF16)

    x_stage(u, x1[...], x2[...], emit)


def view_count(coverage):
    block = strip_index() * ROWS // BLOCK
    count = coverage[0, block, 0]
    for w in range(1, VIEWS):
        count = count + coverage[w, block, 0]
    return count.astype(F32)


def weighted_total(terms, zb, x1b, x2b, hl):
    both = VIEWS * WIDTH
    for i, term in enumerate(terms):
        zmat = zb[i, :, 0:PLANES]
        high, low = slice(i * WIDTH, (i + 1) * WIDTH), slice(both + i * WIDTH, both + (i + 1) * WIDTH)
        for u in range(QUARTER // 2):
            at = 2 * u * PLANES
            rhs = jnp.concatenate(
                [term[at : at + PLANES, :], term[at + PLANES : at + 2 * PLANES, :]], axis=1
            )
            o = dot(zmat, rhs)
            zh, zl = split(o[0:PLANES] + o[PLANES : 2 * PLANES])
            hl[at : at + PLANES, high] = zh[:, 0:WIDTH]
            hl[at : at + PLANES, low] = zl[:, 0:WIDTH]
            at = at + PLANES
            hl[at : at + PLANES, high] = zh[:, WIDTH : 2 * WIDTH]
            hl[at : at + PLANES, low] = zl[:, WIDTH : 2 * WIDTH]
    return dot(hl[...], x1b[...]) + dot(hl[:, 0:both], x2b[...])


def updated(old, acc, count, new):
    for r in range(QUARTER):
        at = pl.ds(r, PLANES, stride=QUARTER)
        new[at, :] = old[at, :] * acc[r * PLANES : (r + 1) * PLANES, :] / count


def first_update_kernel(
    t0, t1, t2, t3, coverage, mine, theirs, zb, x1b, x2b, field, sent, hl, fq
):
    g = lax.axis_index("gz")
    half = QFLAT // 2

    @pl.when(g == 0)
    def _():
        fq[0:half, :] = mine[...]
        fq[half:QFLAT, :] = theirs[...]

    @pl.when(g == 1)
    def _():
        fq[half:QFLAT, :] = mine[...]
        fq[0:half, :] = theirs[...]

    acc = weighted_total((t0, t1, t2, t3), zb, x1b, x2b, hl)
    updated(fq, acc, view_count(coverage), field)
    sent[...] = field[...].reshape(PLANES, QUARTER, WIDTH).astype(BF16)


def as_rows(x):
    return x[...].astype(F32).reshape(QFLAT, WIDTH)


def last_update_kernel(t0, t1, t2, t3, coverage, old, sent, zb, x1b, x2b, coded, hl, new):
    acc = weighted_total((t0, t1, t2, t3), zb, x1b, x2b, hl)
    updated(old, acc, view_count(coverage), new)
    known = as_rows(sent)

    def total(x):
        return jnp.sum(jnp.sum(x, axis=0, keepdims=True), axis=1, keepdims=True)

    scale = total(new[...] * known) / jnp.maximum(total(known * known), 1e-30)
    scale = scale.astype(BF16).astype(F32)
    coded[0:QFLAT, :] = new[...] - scale * known
    coded[QFLAT : QFLAT + TAIL, :] = jnp.broadcast_to(scale, (TAIL, WIDTH))


def decoded(coded, known, at, lines):
    scale = coded[QFLAT : QFLAT + 1, :]
    value = known[at].astype(F32)
    return coded[lines, :].reshape(value.shape) + scale.reshape(1, 1, WIDTH) * value


def halves_kernel(p0, p1, p2, p3, s0, s1, s2, s3, give):
    g = lax.axis_index("gz")
    half = PLANES // 2
    at = pl.ds((1 - g) * half, half)
    lines = pl.ds(pl.multiple_of((1 - g) * half * QUARTER, half * QUARTER), half * QUARTER)
    for j, (ref, sent) in enumerate(((p0, s0), (p1, s1), (p2, s2), (p3, s3))):
        give[j] = decoded(ref, sent, at, lines)


def final_kernel(p0, p1, p2, p3, s0, s1, s2, s3, got, out):
    v, g = lax.axis_index("view"), lax.axis_index("gz")
    half = PLANES // 2
    at = pl.ds(g * half, half)
    lines = pl.ds(pl.multiple_of(g * half * QUARTER, half * QUARTER), half * QUARTER)
    for j, (ref, sent) in enumerate(((p0, s0), (p1, s1), (p2, s2), (p3, s3))):
        q = lax.rem(v - j + VIEWS, VIEWS) * QUARTER
        here = pl.multiple_of(g * ROWS + q, QUARTER)
        there = pl.multiple_of((1 - g) * ROWS + q, QUARTER)
        out[:, pl.ds(here, QUARTER), :] = decoded(ref, sent, at, lines)
        out[:, pl.ds(there, QUARTER), :] = got[j]


def steps(count, shift):
    return [(i, (i + shift) % count) for i in range(count)]


def on_device(estimate, views, shifts, kernels, coverage):
    strips = lax.axis_size("xy")
    count = 2 * strips
    half = PLANES // 2
    quart = (QFLAT, WIDTH)
    strip = arr((PLANES, ROWS, WIDTH), BF16)
    both = [kernels[0], kernels[0][:, ::-1]]
    taps = jnp.pad(jnp.concatenate(both, axis=0), ((0, 2), (0, WIDTH - kernels.shape[2])))

    piece = arr((half, ROWS, WIDTH), BF16)
    eighth = arr((half, QUARTER, WIDTH), F32)
    eb, em, eo, mine, theirs = call(
        prep_estimate_kernel,
        [arr((half, 2 * ROWS, WIDTH), BF16), piece, piece, eighth, eighth],
    )(estimate)
    vm, vo = call(prep_views_kernel, [piece, piece])(views)

    outward, inward = [], []
    for s in range(strips):
        outward += [(2 * s, 2 * ((s + 1) % strips)), (2 * s + 1, 2 * ((s - 1) % strips) + 1)]
        inward += [(2 * s, 2 * ((s - 1) % strips) + 1), (2 * s + 1, 2 * ((s + 1) % strips))]
    swap = steps(2, 1)
    e_far = [lax.ppermute(eo, STRIPS, outward), lax.ppermute(em, STRIPS, inward)]
    e_all = [eb, lax.ppermute(eb, "gz", swap)] + e_far
    v_inside = lax.ppermute(views[0], "gz", swap)
    v_far = [lax.ppermute(vo, STRIPS, outward), lax.ppermute(vm, STRIPS, inward)]
    v_all = [views[0], v_inside] + v_far

    yw, yf, yb, zf, x1f, x2f, yd, xd = call(
        own_mats_kernel,
        [
            arr((2 * ROWS, WIDTH), BF16),
            arr((2 * ROWS, WIDTH), BF16),
            arr((2 * ROWS, WIDTH), BF16),
            arr((2 * PLANES, WIDTH), BF16),
            arr((2 * WIDTH, WIDTH), BF16),
            arr((WIDTH, WIDTH), BF16),
            arr((ROWS, WIDTH), BF16),
            arr((WIDTH, WIDTH), BF16),
        ],
        smem=(1,),
    )(taps, shifts)

    window = pltpu.VMEM((PLANES, SPAN, WIDTH), BF16)
    shifted = pltpu.VMEM((PLANES + 2 * SHIFT, ROWS, WIDTH), BF16)
    flat = pltpu.VMEM((FLAT, WIDTH), F32)
    cube = pltpu.VMEM((PLANES, ROWS, WIDTH), F32)
    pairs = pltpu.VMEM((QFLAT, 2 * VIEWS * WIDTH), BF16)
    total = pltpu.VMEM(quart, F32)

    pred = call(first_pred_kernel, arr((FLAT, WIDTH), F32), [window, flat, flat])(
        *e_all, yw, zf, x1f, x2f
    )
    data, ratio = call(first_ratio_kernel, [strip, strip], [window, shifted], smem=(6,))(
        *v_all, yd, xd, shifts, pred
    )

    across = [(i, (i + 1 if i % 2 else i - 1) % count) for i in range(count)]

    def neighbours(x):
        return lax.ppermute(x, STRIPS, across), lax.ppermute(x, "gz", swap)

    def from_views(x):
        return [x] + [lax.ppermute(x, "view", steps(VIEWS, i)) for i in range(1, VIEWS)]

    late, theirs, _ = lax.optimization_barrier((taps, theirs, ratio))
    theirs = lax.ppermute(theirs, "gz", swap)
    every = from_views(late)
    zb, x1b, x2b = call(
        all_mats_kernel,
        [
            arr((VIEWS, 2 * PLANES, WIDTH), BF16),
            arr((2 * VIEWS * WIDTH, WIDTH), BF16),
            arr((VIEWS * WIDTH, WIDTH), BF16),
        ],
        smem=(4,),
    )(*every, coverage)

    field = None
    for step in range(ITERS):
        far, near = neighbours(ratio)
        parts = call(back_y_kernel, [arr(quart, BF16)] * VIEWS, [flat])(
            far, ratio, near, yb, *(every[1:] if step == 0 else ())
        )
        terms = [parts[0]] + [
            lax.ppermute(parts[i], "view", steps(VIEWS, i)) for i in range(1, VIEWS)
        ]
        if step == 0:
            field, sent = call(
                first_update_kernel,
                [arr(quart, F32), arr((PLANES, QUARTER, WIDTH), BF16)],
                [pairs, total],
                smem=(4,),
            )(
                *terms,
                coverage,
                mine.reshape(QFLAT // 2, WIDTH),
                theirs.reshape(QFLAT // 2, WIDTH),
                zb,
                x1b,
                x2b,
            )
            beyond = lax.ppermute(sent, STRIPS, across)
            sent = from_views(sent)
            outer = from_views(beyond)
            own = call(compose_kernel, strip, [cube])(*sent)
            near = lax.ppermute(own, "gz", swap)
            far = call(compose_kernel, strip, [cube])(*outer)
            ratio = call(next_ratio_kernel, strip, [flat, flat])(
                far, own, near, yf, zf, x1f, x2f, data
            )
        else:
            coded = call(
                last_update_kernel,
                arr((QFLAT + TAIL, WIDTH), F32),
                [pairs, total],
                smem=(4,),
            )(*terms, coverage, field, sent[0], zb, x1b, x2b)
    coded = lax.optimization_barrier(coded.astype(F16))
    pieces = [lax.optimization_barrier(x).astype(F32) for x in from_views(coded)]
    give = call(halves_kernel, arr((VIEWS, half, QUARTER, WIDTH), F32))(*pieces, *sent)
    got = lax.ppermute(give, "gz", swap)
    return call(final_kernel, arr((half, 2 * ROWS, WIDTH), F32))(*pieces, *sent, got)


def solution(mesh):
    placed = (
        P("gz", "xy", None),
        P("view", "gz", "xy", None),
        P("view", None),
        P("view", None, None),
        P(),
    )
    return jax.shard_map(
        on_device, mesh=mesh, in_specs=placed, out_specs=P("gz", "xy", None), check_vma=False
    )
```

```python
import jax
import jax.numpy as jnp
from jax import lax
from jax.experimental import pallas as pl
from jax.experimental.pallas import tpu as pltpu
from jax.sharding import PartitionSpec as P


F32 = jnp.float32
BF16 = jnp.bfloat16
F16 = jnp.float16
ITERS = 2
VIEWS = 4
PLANES = 64
ROWS = 32
WIDTH = 128
SPAN = 3 * ROWS
QUARTER = ROWS // VIEWS
FLAT = ROWS * PLANES
QFLAT = QUARTER * PLANES
HALF = 31
SHIFT = 32
CHUNK = 512
TAIL = 8
BLOCK = 128
STRIPS = ("xy", "gz")


def dot(a, b):
    return jnp.dot(a, b, preferred_element_type=F32)


def split(x):
    high = x.astype(BF16)
    return high, (x - high.astype(F32)).astype(BF16)


def call(kernel, outs, scratch=(), flops=10**8, smem=()):
    def space(i):
        return pltpu.SMEM if i in smem else pltpu.VMEM

    def run(*args):
        specs = [pl.BlockSpec(memory_space=space(i)) for i in range(len(args))]
        one = not isinstance(outs, (list, tuple))
        shapes = [outs] if one else list(outs)
        made = pl.pallas_call(
            kernel,
            out_shape=shapes,
            in_specs=specs,
            out_specs=[pl.BlockSpec(memory_space=pltpu.VMEM)] * len(shapes),
            scratch_shapes=list(scratch),
            compiler_params=pltpu.CompilerParams(vmem_limit_bytes=16 << 20),
            cost_estimate=pl.CostEstimate(flops=flops, bytes_accessed=4 << 20, transcendentals=0),
        )(*args)
        return made[0] if one else made

    return run


def loop(count, body):
    for c in range(count):
        body(c)


def arr(shape, dtype):
    return jax.ShapeDtypeStruct(shape, dtype)


def strip_index():
    return lax.axis_index("xy") * 2 + lax.axis_index("gz")


def prep_estimate_kernel(est, eb, em, eo, mine, theirs):
    v, g = lax.axis_index("view"), lax.axis_index("gz")
    eb[...] = est[...].astype(BF16)

    @pl.when(g == 0)
    def _():
        em[...] = est[:, 0:ROWS, :].astype(BF16)
        eo[...] = est[:, ROWS : 2 * ROWS, :].astype(BF16)

    @pl.when(g == 1)
    def _():
        eo[...] = est[:, 0:ROWS, :].astype(BF16)
        em[...] = est[:, ROWS : 2 * ROWS, :].astype(BF16)

    here = pl.multiple_of(g * ROWS + v * QUARTER, QUARTER)
    there = pl.multiple_of((1 - g) * ROWS + v * QUARTER, QUARTER)
    mine[...] = est[:, pl.ds(here, QUARTER), :]
    theirs[...] = est[:, pl.ds(there, QUARTER), :]


def prep_views_kernel(views, vm, vo):
    g = lax.axis_index("gz")

    @pl.when(g == 0)
    def _():
        vm[...] = views[0, :, 0:ROWS, :]
        vo[...] = views[0, :, ROWS : 2 * ROWS, :]

    @pl.when(g == 1)
    def _():
        vo[...] = views[0, :, 0:ROWS, :]
        vm[...] = views[0, :, ROWS : 2 * ROWS, :]


def toeplitz(row, rows, shift):
    return pltpu.roll(jnp.broadcast_to(row, (rows, WIDTH)), shift, 1, stride=1, stride_axis=0)


def normed(taps):
    return taps / jnp.sum(taps, axis=1, keepdims=True)


def x_matrix(row):
    i = lax.broadcasted_iota(jnp.int32, (WIDTH, WIDTH), 0)
    j = lax.broadcasted_iota(jnp.int32, (WIDTH, WIDTH), 1)
    full = toeplitz(row, WIDTH, WIDTH - HALF)
    return jnp.where(jnp.abs(i - j) <= HALF, full, 0.0)


def row_valid(rows):
    r = strip_index()
    j = lax.broadcasted_iota(jnp.int32, (rows, WIDTH), 1)
    low = jnp.where(r == 0, ROWS, 0)
    high = jnp.where(r == 2 * lax.axis_size("xy") - 1, 2 * ROWS, SPAN)
    return (j >= low) & (j < high)


def own_mats_kernel(taps, shifts, yw, yf, yb, zf, x1f, x2f, yd, xd):
    k = normed(taps[...])
    valid = row_valid(ROWS)
    column = lax.broadcasted_iota(jnp.int32, (ROWS, WIDTH), 1)
    kept = (lax.axis_index("gz") == 0) | ((column >= ROWS) & (column < 2 * ROWS))

    def sides(y):
        return jnp.where(kept, y, pltpu.roll(y, 2 * ROWS, 1))

    forward = jnp.where(valid, toeplitz(k[1:2], ROWS, 1), 0.0)
    backward = jnp.where(valid, toeplitz(k[4:5], ROWS, 1), 0.0)
    for ref, y in ((yw, forward), (yf, sides(forward)), (yb, sides(backward))):
        h, l = split(y)
        ref[0:ROWS, :] = h
        ref[ROWS : 2 * ROWS, :] = l
    lane = lax.broadcasted_iota(jnp.int32, (PLANES, WIDTH), 1)
    z = jnp.where(lane < PLANES, toeplitz(k[0:1], PLANES, WIDTH - HALF), 0.0)
    zh = z.astype(BF16).astype(F32)
    zf[0:PLANES, :] = (zh + pltpu.roll(zh, PLANES, 1)).astype(BF16)
    zf[PLANES : 2 * PLANES, :] = (z - zh).astype(BF16)
    h, l = split(x_matrix(k[5:6]))
    x1f[0:WIDTH, :] = h
    x1f[WIDTH : 2 * WIDTH, :] = h
    x2f[...] = l

    def hot(rows, offset):
        i = lax.broadcasted_iota(jnp.int32, (rows, WIDTH), 0)
        j = lax.broadcasted_iota(jnp.int32, (rows, WIDTH), 1)
        return jnp.where(j - i == offset, 1.0, 0.0)

    yd[...] = jnp.where(valid, hot(ROWS, shifts[0, 1] + ROWS), 0.0).astype(BF16)
    xd[...] = hot(WIDTH, -shifts[0, 2]).astype(BF16)


def all_mats_kernel(t0, t1, t2, t3, coverage, zb, x1b, x2b):
    v = lax.axis_index("view")
    block = strip_index() * ROWS // BLOCK
    for i, taps in enumerate((t0, t1, t2, t3)):
        k = normed(taps[...])
        zh, zl = split(toeplitz(k[3:4], PLANES, WIDTH - HALF))
        zb[i, 0:PLANES, :] = zh
        zb[i, PLANES : 2 * PLANES, :] = zl
        weight = coverage[lax.rem(v - i + VIEWS, VIEWS), block, 0].astype(F32)
        h, l = split(weight * x_matrix(k[2:3]))
        at = slice(i * WIDTH, (i + 1) * WIDTH)
        x1b[at, :] = h
        x1b[VIEWS * WIDTH + i * WIDTH : VIEWS * WIDTH + (i + 1) * WIDTH, :] = h
        x2b[at, :] = l


def y_stage(pair, matrix, put):
    loop(PLANES // 2, lambda c: put(2 * c, dot(matrix, pair(2 * c))))


def filtered_rows(t):
    def put(p, o):
        o = o[0:ROWS] + o[ROWS : 2 * ROWS]
        t[pl.ds(p * ROWS, ROWS), :] = o[:, 0:WIDTH]
        t[pl.ds(p * ROWS + ROWS, ROWS), :] = o[:, WIDTH : 2 * WIDTH]

    return put


def z_stage(t, u, zf):
    def body(c):
        first, second = (pl.ds(2 * c + k, PLANES, stride=ROWS) for k in (0, 1))
        h0, l0 = split(t[first, :])
        h1, l1 = split(t[second, :])
        rhs = jnp.concatenate(
            [jnp.concatenate([h0, h1], axis=1), jnp.concatenate([l0, l1], axis=1)], axis=0
        )
        o = dot(zf, rhs)
        o = o[0:PLANES] + o[PLANES : 2 * PLANES]
        u[first, :] = o[:, 0:WIDTH]
        u[second, :] = o[:, WIDTH : 2 * WIDTH]

    loop(ROWS // 2, body)


def x_stage(t, x1, x2, emit):
    def body(c):
        h, l = split(t[pl.ds(c * CHUNK, CHUNK), :])
        emit(c, dot(jnp.concatenate([h, l], axis=1), x1) + dot(h, x2))

    loop(FLAT // CHUNK, body)


def gather_first(f, slab, other, far_a, far_b):
    g = lax.axis_index("gz")
    low, high = slice(0, PLANES // 2), slice(PLANES // 2, PLANES)

    @pl.when(g == 0)
    def _():
        f[low, ROWS:SPAN, :] = slab[...]
        f[high, ROWS:SPAN, :] = other[...]
        f[low, 0:ROWS, :] = far_a[...]
        f[high, 0:ROWS, :] = far_b[...]

    @pl.when(g == 1)
    def _():
        f[high, 0 : 2 * ROWS, :] = slab[...]
        f[low, 0 : 2 * ROWS, :] = other[...]
        f[high, 2 * ROWS : SPAN, :] = far_a[...]
        f[low, 2 * ROWS : SPAN, :] = far_b[...]


def window_pair(f):
    return lambda p: jnp.concatenate([f[p], f[p + 1]], axis=1)


def strips_pair(far, own, near):
    def pair(p):
        sides = [jnp.concatenate([ref[p], ref[p + 1]], axis=1) for ref in (far, own, near)]
        return jnp.concatenate(sides, axis=0)

    return pair


def chunk_planes(c):
    return pl.ds(c * (CHUNK // ROWS), CHUNK // ROWS)


def as_planes(x):
    return x.reshape(CHUNK // ROWS, ROWS, WIDTH)


def first_pred_kernel(slab, other, far_a, far_b, yw, zf, x1, x2, pred, f, t, u):
    gather_first(f, slab, other, far_a, far_b)
    y_stage(window_pair(f), yw[:, 0:SPAN], filtered_rows(t))
    z_stage(t, u, zf[...])

    def emit(c, x):
        pred[pl.ds(c * CHUNK, CHUNK), :] = x

    x_stage(u, x1[...], x2[...], emit)


def first_ratio_kernel(slab, other, far_a, far_b, yd, xd, shifts, pred, data, ratio, f, d):
    gather_first(f, slab, other, far_a, far_b)
    d[SHIFT : SHIFT + PLANES] = jnp.zeros((PLANES, ROWS, WIDTH), BF16)
    up = SHIFT - shifts[0, 0]

    def put(p, o):
        o = o.astype(BF16)
        d[p + up] = o[:, 0:WIDTH]
        d[p + 1 + up] = o[:, WIDTH : 2 * WIDTH]

    y_stage(window_pair(f), yd[:, 0:SPAN], put)

    def body(c):
        moved = d[pl.ds(SHIFT + c * (CHUNK // ROWS), CHUNK // ROWS)]
        got = dot(moved.reshape(CHUNK, WIDTH), xd[...])
        data[chunk_planes(c)] = as_planes(got).astype(BF16)
        quot = got / (pred[pl.ds(c * CHUNK, CHUNK), :] + 0.05)
        ratio[chunk_planes(c)] = as_planes(quot).astype(BF16)

    loop(FLAT // CHUNK, body)


def back_y_kernel(far, own, near, yb, *refs):
    o0, o1, o2, o3, t = refs[-5:]
    y_stage(strips_pair(far, own, near), yb[:, 0:SPAN], filtered_rows(t))
    v = lax.axis_index("view")
    for i, out in enumerate((o0, o1, o2, o3)):
        q = lax.rem(v + i, VIEWS) * QUARTER
        for r in range(QUARTER):
            out[r * PLANES : (r + 1) * PLANES, :] = t[
                pl.ds(q + r, PLANES, stride=ROWS), :
            ].astype(BF16)


def compose_kernel(p0, p1, p2, p3, own, c):
    v = lax.axis_index("view")
    for j, ref in enumerate((p0, p1, p2, p3)):
        q = pl.multiple_of(lax.rem(v - j + VIEWS, VIEWS) * QUARTER, QUARTER)
        c[:, pl.ds(q, QUARTER), :] = ref[...].astype(F32)
    own[...] = c[...].astype(BF16)


def next_ratio_kernel(far, own, near, yf, zf, x1, x2, data, ratio, t, u):
    y_stage(strips_pair(far, own, near), yf[:, 0:SPAN], filtered_rows(t))
    z_stage(t, u, zf[...])

    def emit(c, x):
        quot = as_planes(x + 0.05)
        ratio[chunk_planes(c)] = (data[chunk_planes(c)].astype(F32) / quot).astype(BF16)

    x_stage(u, x1[...], x2[...], emit)


def view_count(coverage):
    block = strip_index() * ROWS // BLOCK
    count = coverage[0, block, 0]
    for w in range(1, VIEWS):
        count = count + coverage[w, block, 0]
    return count.astype(F32)


def weighted_total(terms, zb, x1b, x2b, hl):
    both = VIEWS * WIDTH
    for i, term in enumerate(terms):
        zmat = zb[i, :, 0:PLANES]
        high, low = slice(i * WIDTH, (i + 1) * WIDTH), slice(both + i * WIDTH, both + (i + 1) * WIDTH)
        for u in range(QUARTER // 2):
            at = 2 * u * PLANES
            rhs = jnp.concatenate(
                [term[at : at + PLANES, :], term[at + PLANES : at + 2 * PLANES, :]], axis=1
            )
            o = dot(zmat, rhs)
            zh, zl = split(o[0:PLANES] + o[PLANES : 2 * PLANES])
            hl[at : at + PLANES, high] = zh[:, 0:WIDTH]
            hl[at : at + PLANES, low] = zl[:, 0:WIDTH]
            at = at + PLANES
            hl[at : at + PLANES, high] = zh[:, WIDTH : 2 * WIDTH]
            hl[at : at + PLANES, low] = zl[:, WIDTH : 2 * WIDTH]
    return dot(hl[...], x1b[...]) + dot(hl[:, 0:both], x2b[...])


def updated(old, acc, count, new):
    for r in range(QUARTER):
        at = pl.ds(r, PLANES, stride=QUARTER)
        new[at, :] = old[at, :] * acc[r * PLANES : (r + 1) * PLANES, :] / count


def first_update_kernel(
    t0, t1, t2, t3, coverage, mine, theirs, zb, x1b, x2b, field, sent, hl, fq
):
    g = lax.axis_index("gz")
    half = QFLAT // 2

    @pl.when(g == 0)
    def _():
        fq[0:half, :] = mine[...]
        fq[half:QFLAT, :] = theirs[...]

    @pl.when(g == 1)
    def _():
        fq[half:QFLAT, :] = mine[...]
        fq[0:half, :] = theirs[...]

    acc = weighted_total((t0, t1, t2, t3), zb, x1b, x2b, hl)
    updated(fq, acc, view_count(coverage), field)
    sent[...] = field[...].reshape(PLANES, QUARTER, WIDTH).astype(BF16)


def as_rows(x):
    return x[...].astype(F32).reshape(QFLAT, WIDTH)


def last_update_kernel(t0, t1, t2, t3, coverage, old, sent, zb, x1b, x2b, coded, hl, new):
    acc = weighted_total((t0, t1, t2, t3), zb, x1b, x2b, hl)
    updated(old, acc, view_count(coverage), new)
    known = as_rows(sent)

    def total(x):
        return jnp.sum(jnp.sum(x, axis=0, keepdims=True), axis=1, keepdims=True)

    scale = total(new[...] * known) / jnp.maximum(total(known * known), 1e-30)
    scale = scale.astype(BF16).astype(F32)
    coded[0:QFLAT, :] = new[...] - scale * known
    coded[QFLAT : QFLAT + TAIL, :] = jnp.broadcast_to(scale, (TAIL, WIDTH))


def decoded(coded, known, at, lines):
    scale = coded[QFLAT : QFLAT + 1, :]
    value = known[at].astype(F32)
    return coded[lines, :].reshape(value.shape) + scale.reshape(1, 1, WIDTH) * value


def halves_kernel(p0, p1, p2, p3, s0, s1, s2, s3, give):
    g = lax.axis_index("gz")
    half = PLANES // 2
    at = pl.ds((1 - g) * half, half)
    lines = pl.ds(pl.multiple_of((1 - g) * half * QUARTER, half * QUARTER), half * QUARTER)
    for j, (ref, sent) in enumerate(((p0, s0), (p1, s1), (p2, s2), (p3, s3))):
        give[j] = decoded(ref, sent, at, lines)


def final_kernel(p0, p1, p2, p3, s0, s1, s2, s3, got, out):
    v, g = lax.axis_index("view"), lax.axis_index("gz")
    half = PLANES // 2
    at = pl.ds(g * half, half)
    lines = pl.ds(pl.multiple_of(g * half * QUARTER, half * QUARTER), half * QUARTER)
    for j, (ref, sent) in enumerate(((p0, s0), (p1, s1), (p2, s2), (p3, s3))):
        q = lax.rem(v - j + VIEWS, VIEWS) * QUARTER
        here = pl.multiple_of(g * ROWS + q, QUARTER)
        there = pl.multiple_of((1 - g) * ROWS + q, QUARTER)
        out[:, pl.ds(here, QUARTER), :] = decoded(ref, sent, at, lines)
        out[:, pl.ds(there, QUARTER), :] = got[j]


def steps(count, shift):
    return [(i, (i + shift) % count) for i in range(count)]


def on_device(estimate, views, shifts, kernels, coverage):
    strips = lax.axis_size("xy")
    count = 2 * strips
    half = PLANES // 2
    quart = (QFLAT, WIDTH)
    strip = arr((PLANES, ROWS, WIDTH), BF16)
    both = [kernels[0], kernels[0][:, ::-1]]
    taps = jnp.pad(jnp.concatenate(both, axis=0), ((0, 2), (0, WIDTH - kernels.shape[2])))

    piece = arr((half, ROWS, WIDTH), BF16)
    eighth = arr((half, QUARTER, WIDTH), F32)
    eb, em, eo, mine, theirs = call(
        prep_estimate_kernel,
        [arr((half, 2 * ROWS, WIDTH), BF16), piece, piece, eighth, eighth],
    )(estimate)
    vm, vo = call(prep_views_kernel, [piece, piece])(views)

    outward, inward = [], []
    for s in range(strips):
        outward += [(2 * s, 2 * ((s + 1) % strips)), (2 * s + 1, 2 * ((s - 1) % strips) + 1)]
        inward += [(2 * s, 2 * ((s - 1) % strips) + 1), (2 * s + 1, 2 * ((s + 1) % strips))]
    swap = steps(2, 1)
    e_far = [lax.ppermute(eo, STRIPS, outward), lax.ppermute(em, STRIPS, inward)]
    e_all = [eb, lax.ppermute(eb, "gz", swap)] + e_far
    v_inside = lax.ppermute(views[0], "gz", swap)
    v_far = [lax.ppermute(vo, STRIPS, outward), lax.ppermute(vm, STRIPS, inward)]
    v_all = [views[0], v_inside] + v_far

    yw, yf, yb, zf, x1f, x2f, yd, xd = call(
        own_mats_kernel,
        [
            arr((2 * ROWS, WIDTH), BF16),
            arr((2 * ROWS, WIDTH), BF16),
            arr((2 * ROWS, WIDTH), BF16),
            arr((2 * PLANES, WIDTH), BF16),
            arr((2 * WIDTH, WIDTH), BF16),
            arr((WIDTH, WIDTH), BF16),
            arr((ROWS, WIDTH), BF16),
            arr((WIDTH, WIDTH), BF16),
        ],
        smem=(1,),
    )(taps, shifts)

    window = pltpu.VMEM((PLANES, SPAN, WIDTH), BF16)
    shifted = pltpu.VMEM((PLANES + 2 * SHIFT, ROWS, WIDTH), BF16)
    flat = pltpu.VMEM((FLAT, WIDTH), F32)
    cube = pltpu.VMEM((PLANES, ROWS, WIDTH), F32)
    pairs = pltpu.VMEM((QFLAT, 2 * VIEWS * WIDTH), BF16)
    total = pltpu.VMEM(quart, F32)

    pred = call(first_pred_kernel, arr((FLAT, WIDTH), F32), [window, flat, flat])(
        *e_all, yw, zf, x1f, x2f
    )
    data, ratio = call(first_ratio_kernel, [strip, strip], [window, shifted], smem=(6,))(
        *v_all, yd, xd, shifts, pred
    )

    across = [(i, (i + 1 if i % 2 else i - 1) % count) for i in range(count)]

    def neighbours(x):
        return lax.ppermute(x, STRIPS, across), lax.ppermute(x, "gz", swap)

    def from_views(x):
        return [x] + [lax.ppermute(x, "view", steps(VIEWS, i)) for i in range(1, VIEWS)]

    late, theirs, _ = lax.optimization_barrier((taps, theirs, ratio))
    theirs = lax.ppermute(theirs, "gz", swap)
    every = from_views(late)
    zb, x1b, x2b = call(
        all_mats_kernel,
        [
            arr((VIEWS, 2 * PLANES, WIDTH), BF16),
            arr((2 * VIEWS * WIDTH, WIDTH), BF16),
            arr((VIEWS * WIDTH, WIDTH), BF16),
        ],
        smem=(4,),
    )(*every, coverage)

    field = None
    for step in range(ITERS):
        far, near = neighbours(ratio)
        parts = call(back_y_kernel, [arr(quart, BF16)] * VIEWS, [flat])(
            far, ratio, near, yb, *(every[1:] if step == 0 else ())
        )
        terms = [parts[0]]
        for i in range(1, VIEWS):
            terms.append(lax.ppermute(parts[i], "view", steps(VIEWS, i)))
        if step == 0:
            field, sent = call(
                first_update_kernel,
                [arr(quart, F32), arr((PLANES, QUARTER, WIDTH), BF16)],
                [pairs, total],
                smem=(4,),
            )(
                *terms,
                coverage,
                mine.reshape(QFLAT // 2, WIDTH),
                theirs.reshape(QFLAT // 2, WIDTH),
                zb,
                x1b,
                x2b,
            )
            beyond = lax.ppermute(sent, STRIPS, across)
            sent = from_views(sent)
            outer = from_views(beyond)
            own = call(compose_kernel, strip, [cube])(*sent)
            near = lax.ppermute(own, "gz", swap)
            far = call(compose_kernel, strip, [cube])(*outer)
            ratio = call(next_ratio_kernel, strip, [flat, flat])(
                far, own, near, yf, zf, x1f, x2f, data
            )
        else:
            coded = call(
                last_update_kernel,
                arr((QFLAT + TAIL, WIDTH), F32),
                [pairs, total],
                smem=(4,),
            )(*terms, coverage, field, sent[0], zb, x1b, x2b)
    coded = lax.optimization_barrier(coded.astype(F16))
    pieces = [lax.optimization_barrier(x).astype(F32) for x in from_views(coded)]
    give = call(halves_kernel, arr((VIEWS, half, QUARTER, WIDTH), F32))(*pieces, *sent)
    got = lax.ppermute(give, "gz", swap)
    return call(final_kernel, arr((half, 2 * ROWS, WIDTH), F32))(*pieces, *sent, got)


def solution(mesh):
    placed = (
        P("gz", "xy", None),
        P("view", "gz", "xy", None),
        P("view", None),
        P("view", None, None),
        P(),
    )
    return jax.shard_map(
        on_device, mesh=mesh, in_specs=placed, out_specs=P("gz", "xy", None), check_vma=False
    )
```
